256 devices in a mesh: heads: 16 (over x_lo, y, core), keys: 16 (over z, x_hi).
Axes of the slice: x: 4 (x_hi: 2, x_lo: 2; x = x_hi * 2 + x_lo), y: 4, z: 8, core: 2. Of those that a mesh axis runs over, the one named last changes fastest.
Arguments:
- main_query: bfloat16 [256, 128, 576], P(None, 'heads'), may hold values from -5 to 5
- latent_keys: bfloat16 [32768, 576], P('keys'), may hold values from -16 to 16
- index_query: bfloat16 [256, 64, 128], P('heads'), may hold values from -1 to 1
- index_keys: bfloat16 [32768, 128], P('keys'), may hold values from -20 to 20
- index_weight: float32 [256, 64], P('heads'), may hold values from -0.15 to 1
- query_pos: int32 [256], replicated, may hold values from 4096 to 32767, as said below
- kl_weight: float32 [256], P('heads'), may hold values from 2 to 16
Outputs:
- index_query_grad: float32 [256, 64, 128], P('heads')
- index_key_grad: float32 [32768, 128], P('keys')
- index_weight_grad: float32 [256, 64], P('heads')
The draws below stay inside these ranges and needn't reach their ends.
Inputs may be any that keep to these rules, and one draw needn't show every extreme that they name: Query q sees the keys at positions 0 to query_pos[q]; some query sees all 32768 keys and some sees exactly the first 4097.
All inputs are finite; a program needn't handle non-finite values.
Results may differ from the reference program's by a relative error of at most 0.005.
Values sent between devices are 32-bit elements; how exact they have to be, the bound alone decides.
A program may use at most 128 MiB of HBM per device.

```python
import math
import jax
import jax.numpy as jnp
from jax import lax

H = 128
D = 576
HI = 64
DI = 128
QROW_DEV = 16
Q = 256
KEYS = 32768


def row_scales(key, shape, lower, upper):
    return jnp.exp(jax.random.uniform(key, shape, jnp.float32, math.log(lower), math.log(upper)))


def draw_latent_keys(key, part):
    base_key = jax.random.fold_in(key, 101)
    scales = row_scales(jax.random.fold_in(base_key, 1), (KEYS, 1), 0.3, 3.0)
    values = jax.random.truncated_normal(jax.random.fold_in(base_key, 2), -5.0, 5.0, (KEYS, D), jnp.float32) * scales
    return values.astype(jnp.bfloat16)


def draw_main_query(key, part):
    base_key = jax.random.fold_in(key, 102)
    scales = row_scales(jax.random.fold_in(base_key, 1), (Q, H, 1), 0.03, 0.3)
    values = jax.random.truncated_normal(jax.random.fold_in(base_key, 2), -5.0, 5.0, (Q, H, D), jnp.float32) * scales
    return values.astype(jnp.bfloat16)


def draw_index_keys(key, part):
    base_key = jax.random.fold_in(key, 103)
    scales = row_scales(jax.random.fold_in(base_key, 1), (KEYS, 1), 0.4, 4.0)
    values = jax.random.truncated_normal(jax.random.fold_in(base_key, 2), -5.0, 5.0, (KEYS, DI), jnp.float32) * scales
    return values.astype(jnp.bfloat16)


def draw_index_query(key, part):
    base_key = jax.random.fold_in(key, 104)
    values = jax.random.truncated_normal(jax.random.fold_in(base_key, 2), -5.0, 5.0, (Q, HI, DI), jnp.float32) * DI ** (-0.5)
    return values.astype(jnp.bfloat16)


def draw_index_weight(key, part):
    base_key = jax.random.fold_in(key, 105)
    values = jax.random.truncated_normal(jax.random.fold_in(base_key, 2), -5.0, 5.0, (Q, HI), jnp.float32) * 0.03
    return values.astype(jnp.float32)


def draw_query_pos(key, part):
    values = jax.random.randint(jax.random.fold_in(key, 201), (Q,), KEYS // 8, KEYS)
    values = values.at[0].set(KEYS - 1)
    values = values.at[1].set(KEYS // 8)
    return values.astype(jnp.int32)


def level_of(rng, extent, split, smallest, high):
    def one(axis_at, parts):
        heights = jax.random.uniform(jax.random.fold_in(jax.random.fold_in(rng, 6), axis_at), (parts,), jnp.float32, smallest / len(split), high / len(split))
        return jnp.repeat(jnp.exp(heights), extent[axis_at] // parts).reshape((-1,) + (1,) * (len(extent) - axis_at - 1))

    level = one(*split[0])
    for cut in split[1:]:
        level = level * one(*cut)
    return level


def setup_inputs(seed: int = 0) -> dict:
    key_of = jax.random.split(jax.random.key(seed), 8)
    return {
        "main_query": draw_main_query(jax.random.fold_in(key_of[7], 71), 0),
        "latent_keys": draw_latent_keys(jax.random.fold_in(key_of[7], 71), 0),
        "index_query": draw_index_query(jax.random.fold_in(key_of[7], 71), 0),
        "index_keys": draw_index_keys(jax.random.fold_in(key_of[7], 71), 0),
        "index_weight": draw_index_weight(jax.random.fold_in(key_of[7], 71), 0),
        "query_pos": draw_query_pos(jax.random.fold_in(key_of[7], 71), 0),
        "kl_weight": jnp.clip(jnp.exp(math.log(16.0) - 2.0794415 * jax.random.uniform(key_of[6], (Q,), jnp.float32) ** level_of(key_of[6], (Q,), ((0, 16),), -0.2, 0.2)), 2.0, 16.0),
    }


softmax_scale = 192.0 ** -0.5
masked_fill = -1e30


def reference(main_query, latent_keys, index_query, index_keys, index_weight, query_pos, kl_weight):
    key_index = jnp.arange(KEYS, dtype=jnp.int32)
    visible = key_index[None, :] <= query_pos[:, None].astype(jnp.int32)
    query_total = query_pos.shape[0]

    def head_step(summed, query_head):
        scores = jnp.dot(query_head, latent_keys.T, preferred_element_type=jnp.float32) * softmax_scale
        scores = jnp.where(visible, scores, masked_fill)
        maxima = jnp.max(scores, axis=1, keepdims=True)
        weights = jnp.where(visible, jnp.exp(scores - maxima), 0.0)
        return summed + weights / jnp.sum(weights, axis=1, keepdims=True), None

    summed, _ = lax.scan(head_step, jnp.zeros((query_total, KEYS), jnp.float32), jnp.swapaxes(main_query, 0, 1))
    target = summed / H

    blocks = query_total // QROW_DEV

    def block_step(key_grad, inputs):
        query_block, weight_block, visible_block, target_block, kl_block = inputs
        logits = jnp.dot(query_block.reshape(QROW_DEV * HI, DI), index_keys.T, preferred_element_type=jnp.float32)
        logits = logits.reshape(QROW_DEV, HI, KEYS)
        active = jnp.maximum(logits, 0.0)
        iscores = jnp.einsum("qj,qjk->qk", weight_block, active, precision=lax.Precision.HIGHEST)
        iscores = jnp.where(visible_block, iscores, masked_fill)
        maxima = jnp.max(iscores, axis=1, keepdims=True)
        weights = jnp.where(visible_block, jnp.exp(iscores - maxima), 0.0)
        iprobs = weights / jnp.sum(weights, axis=1, keepdims=True)
        delta = kl_block[:, None] * (iprobs - target_block)
        weight_grad = jnp.einsum("qk,qjk->qj", delta, active, precision=lax.Precision.HIGHEST)
        slopes = jnp.where(logits > 0.0, delta[:, None, :] * weight_block[:, :, None], 0.0).astype(jnp.bfloat16)
        flattened = slopes.reshape(QROW_DEV * HI, KEYS)
        query_grad = jnp.dot(flattened, index_keys, preferred_element_type=jnp.float32).reshape(QROW_DEV, HI, DI)
        key_part = lax.dot_general(flattened, query_block.reshape(QROW_DEV * HI, DI), (((0,), (0,)), ((), ())), preferred_element_type=jnp.float32)
        return key_grad + key_part, (query_grad, weight_grad)

    inputs = (
        index_query.reshape(blocks, QROW_DEV, HI, DI),
        index_weight.reshape(blocks, QROW_DEV, HI),
        visible.reshape(blocks, QROW_DEV, KEYS),
        target.reshape(blocks, QROW_DEV, KEYS),
        kl_weight.reshape(blocks, QROW_DEV),
    )
    key_grad, (query_grad, weight_grad) = lax.scan(block_step, jnp.zeros((KEYS, DI), jnp.float32), inputs)
    return query_grad.reshape(query_total, HI, DI), key_grad, weight_grad.reshape(query_total, HI)
```

```python
import jax
import jax.numpy as jnp
from jax import lax
from jax.experimental import pallas as pl
from jax.experimental.pallas import tpu as pltpu
from jax.sharding import PartitionSpec as P

H = 128
SCALE = 192.0 ** (-0.5)
MASKED = -1e30
FLOOR = -1e29
MESH = pl.DeviceIdType.MESH
LAG = 3
NT = (((1,), (1,)), ((), ()))
F32 = jnp.float32
BF16 = jnp.bfloat16


def lanes(t):
    return slice(t * 128, (t + 1) * 128)


def fused(
    pos_s, kl_s, mq, lk, iq, ik, iw,
    qg_out, kg_out, wg_out,
    s_ref, e_ref, st_ref, stat_mine, stat_all,
    tp_ref, tc_ref, tx_ref, ty_ref,
    lg_ref, wpad_ref, wcol_ref, iqt_ref, is_ref, ie_ref, ist_mine, ist_all, d_ref,
    sl_ref, wgc_ref, qg_part, qg_recv, qg_xh, qg_all,
    kp_ref, kc_ref, kx_ref, ky_ref, kg_all,
    stat_ss, stat_rs, ist_ss, ist_rs,
    tc_ss, tc_rs, tx_ss, tx_rs, ty_ss, ty_rs,
    qg_ss, qg_rs, xh_ss, xh_rs, qa_ss, qa_rs,
    kc_ss, kc_rs, kx_ss, kx_rs, ky_ss, ky_rs, ka_ss, ka_rs,
):
    h = lax.axis_index("heads")
    k = lax.axis_index("keys")
    core, y, x = h % 2, (h // 2) % 4, h // 8
    z, xh = k // 2, k % 2
    key_first = k * 2048
    partner = x * 8 + y * 2 + (1 - core)
    across = (1 - x) * 8 + y * 2 + core

    def along_y(off):
        return x * 8 + ((y + off) % 4) * 2 + core

    def chip(b):
        return ((x + 1 - b // 4) % 2) * 4 + (y + 3 - b % 4) % 4

    barrier = pltpu.get_barrier_semaphore()
    for r in range(1, 16):
        pl.semaphore_signal(barrier, inc=1, device_id={"keys": (k + r) % 16}, device_id_type=MESH)
    for peer in (partner, across, along_y(1), along_y(2), along_y(3)):
        pl.semaphore_signal(barrier, inc=1, device_id={"heads": peer}, device_id_type=MESH)

    lane = lax.broadcasted_iota(jnp.int32, (1, 128), 1)

    wpad_ref[...] = jnp.zeros((128, 128), F32)
    wpad_ref[0:16, 0:64] = iw[...]
    wturned = jnp.transpose(wpad_ref[...])
    for q in range(16):
        wcol_ref[q * 64:(q + 1) * 64, :] = jnp.broadcast_to(wturned[0:64, q:q + 1], (64, 128))
    for i in range(8):
        iqt_ref[:, lanes(i)] = jnp.transpose(iq[lanes(i), :].astype(F32)).astype(BF16)

    def to_heads(src, dst, ss, rs, peer):
        return pltpu.make_async_remote_copy(
            src_ref=src, dst_ref=dst, send_sem=ss, recv_sem=rs,
            device_id={"heads": peer}, device_id_type=MESH,
        )

    def to_keys(src, dst, ss, rs, peer):
        return pltpu.make_async_remote_copy(
            src_ref=src, dst_ref=dst, send_sem=ss, recv_sem=rs,
            device_id={"keys": peer}, device_id_type=MESH,
        )

    def take(ref, sem):
        pltpu.make_async_copy(ref, ref, sem).wait()

    def score_block(b):
        c = chip(b)
        r0 = pl.multiple_of(c * 256, 256)
        s_ref[...] = lax.dot_general(mq[pl.ds(r0, 256), :], lk[...], NT, preferred_element_type=F32)

        def piece(i, carry):
            rows = pl.ds(pl.multiple_of(i * 64, 64), 64)
            posv = jnp.concatenate(
                [jnp.full((8, 128), pos_s[c * 32 + i * 8 + j] - key_first, jnp.int32) for j in range(8)],
                axis=0,
            )
            top = jnp.full((64, 128), FLOOR, F32)
            for t in range(16):
                v = jnp.where(lane + t * 128 <= posv, s_ref[rows, lanes(t)], MASKED)
                s_ref[rows, lanes(t)] = v
                top = jnp.maximum(top, v)
            mcol = jnp.broadcast_to(jnp.max(top, axis=1, keepdims=True), (64, 128))
            total = jnp.zeros((64, 128), F32)
            erows = pl.ds(pl.multiple_of(r0 + i * 64, 64), 64)
            for t in range(16):
                e = jnp.exp((s_ref[rows, lanes(t)] - mcol) * SCALE)
                total = total + e
                e_ref[erows, lanes(t)] = e.astype(BF16)
            lcol = jnp.broadcast_to(jnp.sum(total, axis=1, keepdims=True), (64, 128))
            st_ref[rows, :] = jnp.where(lane == 0, mcol, lcol)
            return carry

        lax.fori_loop(0, 4, piece, 0)
        stat_mine[b] = jnp.transpose(st_ref[...])[0:2, :]

    def send_stats(b):
        for r in range(1, 16):
            to_keys(stat_mine.at[b], stat_all.at[b, r - 1], stat_ss.at[b], stat_rs.at[b], (k + r) % 16).start()

    def target_block(b):
        take(stat_all.at[b], stat_rs.at[b])
        mine = stat_mine[b]
        m0, l0 = mine[0:1, :], mine[1:2, :]
        ms = [stat_all[b, r][0:1, :] for r in range(15)]
        ls = [stat_all[b, r][1:2, :] for r in range(15)]
        top = m0
        for m in ms:
            top = jnp.maximum(top, m)
        share = jnp.exp((m0 - top) * SCALE)
        total = l0 * share
        for m, l in zip(ms, ls):
            total = total + l * jnp.exp((m - top) * SCALE)
        w = share / (total * float(H))
        high = w.astype(BF16).astype(F32)
        low = w - high
        mine_of = lax.broadcasted_iota(jnp.int32, (32, 256), 1) // 8 == lax.broadcasted_iota(
            jnp.int32, (32, 256), 0
        )
        a = jnp.concatenate([jnp.where(mine_of, high, 0.0), jnp.where(mine_of, low, 0.0)], axis=0)
        r0 = pl.multiple_of(chip(b) * 256, 256)
        got = jnp.dot(a.astype(BF16), e_ref[pl.ds(r0, 256), :], preferred_element_type=F32)
        got = got[0:32, :] + got[32:64, :]
        tp_ref[b, 0] = got[0:16, :]
        tp_ref[b, 1] = got[16:32, :]
        to_heads(tp_ref.at[b, 1 - core], tc_ref.at[b], tc_ss.at[b], tc_rs.at[b], partner).start()

    def cross_x(b, p_ref, c_ref, x_ref, c_rs, x_ss, x_rs):
        take(c_ref.at[b], c_rs.at[b])
        p_ref[b, core] = p_ref[b, core] + c_ref[b]
        to_heads(p_ref.at[b, core], x_ref.at[b], x_ss.at[b], x_rs.at[b], across).start()

    def cross_y(i, p_ref, c_ref, x_ref, y_ref, c_rs, x_rs, y_ss, y_rs):
        b = 4 + i
        take(c_ref.at[b], c_rs.at[b])
        take(x_ref.at[i], x_rs.at[i])
        p_ref[b, core] = p_ref[b, core] + c_ref[b] + x_ref[i]
        off = 3 - i
        if off:
            to_heads(
                p_ref.at[b, core], y_ref.at[off - 1], y_ss.at[off - 1], y_rs.at[off - 1], along_y(off)
            ).start()

    score_block(0)
    pl.semaphore_wait(barrier, 20)
    send_stats(0)

    def main_step(b, carry):
        score_block(b)
        send_stats(b)

        @pl.when(b >= LAG)
        def _():
            target_block(b - LAG)

        @pl.when(b >= LAG + 1)
        def _():
            cross_x(b - LAG - 1, tp_ref, tc_ref, tx_ref, tc_rs, tx_ss, tx_rs)

        return carry

    lax.fori_loop(1, 8, main_step, 0)

    sub = lax.broadcasted_iota(jnp.int32, (8, 128), 0)
    is_ref[...] = jnp.zeros((16, 2048), F32)

    def index_step(g, carry):
        rows = pl.ds(pl.multiple_of(g * 256, 256), 256)
        lg_ref[rows, :] = lax.dot_general(iq[rows, :], ik[...], NT, preferred_element_type=F32)

        def one(j, inner):
            q = g * 4 + j
            qrows = pl.ds(pl.multiple_of(q * 64, 64), 64)
            w = wcol_ref[qrows, :]
            eight = pl.ds(pl.multiple_of((q // 8) * 8, 8), 8)
            for t in range(16):
                got = jnp.sum(jnp.maximum(lg_ref[qrows, lanes(t)], 0.0) * w, axis=0, keepdims=True)
                is_ref[eight, lanes(t)] = jnp.where(
                    sub == q % 8, jnp.broadcast_to(got, (8, 128)), is_ref[eight, lanes(t)]
                )
            return inner

        lax.fori_loop(0, 4, one, 0)

        @pl.when(g < LAG)
        def _():
            target_block(8 - LAG + g)

        return carry

    lax.fori_loop(0, 4, index_step, 0)

    row = lax.broadcasted_iota(jnp.int32, (16, 128), 0)
    posr = jnp.zeros((16, 128), jnp.int32)
    klr = jnp.zeros((16, 128), F32)
    for q in range(16):
        posr = jnp.where(row == q, pos_s[h * 16 + q] - key_first, posr)
        klr = jnp.where(row == q, kl_s[q], klr)
    top = jnp.full((16, 128), FLOOR, F32)
    for t in range(16):
        v = jnp.where(lane + t * 128 <= posr, is_ref[:, lanes(t)], MASKED)
        is_ref[:, lanes(t)] = v
        top = jnp.maximum(top, v)
    im = jnp.broadcast_to(jnp.max(top, axis=1, keepdims=True), (16, 128))
    total = jnp.zeros((16, 128), F32)
    for t in range(16):
        e = jnp.exp(is_ref[:, lanes(t)] - im)
        total = total + e
        ie_ref[:, lanes(t)] = e
    il = jnp.broadcast_to(jnp.sum(total, axis=1, keepdims=True), (16, 128))
    ist_mine[...] = jnp.where(lane == 0, im, il)
    for r in range(1, 16):
        to_keys(ist_mine, ist_all.at[r - 1], ist_ss, ist_rs, (k + r) % 16).start()

    for i in range(4):
        cross_y(i, tp_ref, tc_ref, tx_ref, ty_ref, tc_rs, tx_rs, ty_ss, ty_rs)

    take(ist_all, ist_rs)
    ms = [jnp.broadcast_to(ist_all[r][:, 0:1], (16, 128)) for r in range(15)]
    top = im
    for m in ms:
        top = jnp.maximum(top, m)
    share = jnp.exp(im - top)
    total = il * share
    for r in range(15):
        total = total + jnp.broadcast_to(ist_all[r][:, 1:2], (16, 128)) * jnp.exp(ms[r] - top)
    share = share / total

    for j in range(3):
        take(ty_ref.at[j], ty_rs.at[j])
    for t in range(16):
        target = tp_ref[7, core, :, lanes(t)]
        for j in range(3):
            target = target + ty_ref[j, :, lanes(t)]
        delta = klr * (ie_ref[:, lanes(t)] * share - target)
        for q in range(16):
            d_ref[q, :, lanes(t)] = jnp.broadcast_to(delta[q:q + 1, :], (8, 128))

    def back_step(n, carry):
        g = (z // 2 + 1 + n) % 4
        wgc_ref[...] = jnp.zeros((128, 128), F32)

        def one(j, inner):
            q = g * 4 + j
            qrows = pl.ds(pl.multiple_of(q * 64, 64), 64)
            w = wcol_ref[qrows, :]
            acc = jnp.zeros((64, 128), F32)
            for t in range(16):
                d = jnp.concatenate([d_ref[q, :, lanes(t)]] * 8, axis=0)
                v = lg_ref[qrows, lanes(t)]
                sl_ref[qrows, lanes(t)] = jnp.where(v > 0.0, d * w, 0.0).astype(BF16)
                acc = acc + jnp.maximum(v, 0.0) * d
            col = jnp.broadcast_to(jnp.sum(acc, axis=1, keepdims=True), (64, 128))
            at = (j // 2) * 8 + j % 2
            wgc_ref[0:64, :] = jnp.where(lane == at, col, wgc_ref[0:64, :])
            return inner

        lax.fori_loop(0, 4, one, 0)
        turned = jnp.transpose(wgc_ref[...])
        rows = pl.ds(pl.multiple_of(g * 256, 256), 256)
        got = jnp.dot(sl_ref[rows, :], ik[...], preferred_element_type=F32)
        for j in range(2):
            blk = g * 2 + j
            qg_part[blk, 0:128, :] = got[j * 128:(j + 1) * 128, :]
            qg_part[blk, 128:136, :] = turned[j * 8:(j + 1) * 8, :]
            r = (blk - z + 8) % 8

            @pl.when(r > 0)
            def _():
                to_keys(
                    qg_part.at[blk], qg_recv.at[r - 1], qg_ss.at[r - 1], qg_rs.at[r - 1], blk * 2 + xh
                ).start()

        return carry

    lax.fori_loop(0, 4, back_step, 0)

    def key_step(b, carry):
        cols = pl.ds(pl.multiple_of(chip(b) * 256, 256), 256)
        got = jnp.dot(iqt_ref[...], sl_ref[:, cols], preferred_element_type=F32)
        kp_ref[b, 0] = got[:, 0:128]
        kp_ref[b, 1] = got[:, 128:256]
        to_heads(kp_ref.at[b, 1 - core], kc_ref.at[b], kc_ss.at[b], kc_rs.at[b], partner).start()

        @pl.when((b >= 1) & (b < 5))
        def _():
            cross_x(b - 1, kp_ref, kc_ref, kx_ref, kc_rs, kx_ss, kx_rs)

        return carry

    lax.fori_loop(0, 8, key_step, 0)

    for j in range(7):
        take(qg_recv.at[j], qg_rs.at[j])
    acc = qg_part[z]
    for j in range(7):
        acc = acc + qg_recv[j]
    qg_part[z] = acc
    to_keys(qg_part.at[z], qg_xh, xh_ss, xh_rs, z * 2 + (1 - xh)).start()

    for i in range(4):
        cross_y(i, kp_ref, kc_ref, kx_ref, ky_ref, kc_rs, kx_rs, ky_ss, ky_rs)

    take(qg_xh, xh_rs)
    qg_all[z] = qg_part[z] + qg_xh[...]
    for r in range(1, 8):
        to_keys(
            qg_all.at[z], qg_all.at[z], qa_ss.at[r - 1], qa_rs.at[r - 1], ((z + r) % 8) * 2 + xh
        ).start()

    for j in range(3):
        take(ky_ref.at[j], ky_rs.at[j])
    shard = kp_ref[7, core]
    for j in range(3):
        shard = shard + ky_ref[j]
    kg_all[h] = jnp.transpose(shard)

    def pass_on(s, peer, n):
        to_heads(kg_all.at[s], kg_all.at[s], ka_ss.at[n], ka_rs.at[s], peer).start()

    for off in (1, 2, 3):
        pass_on(h, along_y(off), off - 1)
    pass_on(h, across, 3)
    pass_on(h, partner, 4)
    for off in (1, 3, 2):
        s = along_y(off)
        take(kg_all.at[s], ka_rs.at[s])
        pass_on(s, across, 4 + off)
        pass_on(s, partner, 7 + off)
    for off in (0, 1, 3, 2):
        s = (1 - x) * 8 + ((y + off) % 4) * 2 + core
        take(kg_all.at[s], ka_rs.at[s])
        pass_on(s, partner, 11 + off)

    for r in range(1, 8):
        take(qg_all.at[(z - r + 8) % 8], qa_rs.at[r - 1])
    for i in range(8):
        qg_out[i * 128:(i + 1) * 128, :] = qg_all[i, 0:128, :]
        wg_out[i * 2:(i + 1) * 2, :] = qg_all[i, 128:130, 0:64]
    for c in range(8):
        s = c * 2 + (1 - core)
        take(kg_all.at[s], ka_rs.at[s])
    for s in range(16):
        kg_out[s * 128:(s + 1) * 128, :] = kg_all[s]

    for b in range(8):
        take(stat_all.at[b], stat_ss.at[b])
        take(tc_ref.at[b], tc_ss.at[b])
        take(kc_ref.at[b], kc_ss.at[b])
    take(ist_all, ist_ss)
    for b in range(4):
        take(tx_ref.at[b], tx_ss.at[b])
        take(kx_ref.at[b], kx_ss.at[b])
    for j in range(3):
        take(ty_ref.at[j], ty_ss.at[j])
        take(ky_ref.at[j], ky_ss.at[j])
    for j in range(7):
        take(qg_recv.at[j], qg_ss.at[j])
        take(qg_all.at[j], qa_ss.at[j])
    take(qg_xh, xh_ss)
    for n in range(15):
        take(kg_all.at[n], ka_ss.at[n])


def shards(main_query, latent_keys, index_query, index_keys, index_weight, query_pos, kl_weight):
    vmem = pl.BlockSpec(memory_space=pltpu.VMEM)
    smem = pl.BlockSpec(memory_space=pltpu.SMEM)
    dma = pltpu.SemaphoreType.DMA
    query_grad, key_grad, weight_grad = pl.pallas_call(
        fused,
        out_shape=(
            jax.ShapeDtypeStruct((1024, 128), F32),
            jax.ShapeDtypeStruct((2048, 128), F32),
            jax.ShapeDtypeStruct((16, 64), F32),
        ),
        in_specs=[smem, smem] + [vmem] * 5,
        out_specs=(vmem, vmem, vmem),
        scratch_shapes=[
            pltpu.VMEM((256, 2048), F32),
            pltpu.VMEM((2048, 2048), BF16),
            pltpu.VMEM((256, 128), F32),
            pltpu.VMEM((8, 2, 256), F32),
            pltpu.VMEM((8, 15, 2, 256), F32),
            pltpu.VMEM((8, 2, 16, 2048), F32),
            pltpu.VMEM((8, 16, 2048), F32),
            pltpu.VMEM((4, 16, 2048), F32),
            pltpu.VMEM((3, 16, 2048), F32),
            pltpu.VMEM((1024, 2048), F32),
            pltpu.VMEM((128, 128), F32),
            pltpu.VMEM((1024, 128), F32),
            pltpu.VMEM((128, 1024), BF16),
            pltpu.VMEM((16, 2048), F32),
            pltpu.VMEM((16, 2048), F32),
            pltpu.VMEM((16, 128), F32),
            pltpu.VMEM((15, 16, 128), F32),
            pltpu.VMEM((16, 8, 2048), F32),
            pltpu.VMEM((1024, 2048), BF16),
            pltpu.VMEM((128, 128), F32),
            pltpu.VMEM((8, 136, 128), F32),
            pltpu.VMEM((7, 136, 128), F32),
            pltpu.VMEM((136, 128), F32),
            pltpu.VMEM((8, 136, 128), F32),
            pltpu.VMEM((8, 2, 128, 128), F32),
            pltpu.VMEM((8, 128, 128), F32),
            pltpu.VMEM((4, 128, 128), F32),
            pltpu.VMEM((3, 128, 128), F32),
            pltpu.VMEM((16, 128, 128), F32),
            dma((8,)), dma((8,)), dma, dma,
            dma((8,)), dma((8,)), dma((4,)), dma((4,)), dma((3,)), dma((3,)),
            dma((7,)), dma((7,)), dma, dma, dma((7,)), dma((7,)),
            dma((8,)), dma((8,)), dma((4,)), dma((4,)), dma((3,)), dma((3,)),
            dma((15,)), dma((16,)),
        ],
        compiler_params=pltpu.CompilerParams(
            collective_id=0, has_side_effects=True, vmem_limit_bytes=60 * 1024 * 1024
        ),
        name="fused_indexer_step",
    )(
        query_pos,
        kl_weight,
        main_query.reshape(2048, 576),
        latent_keys,
        index_query.reshape(1024, 128),
        index_keys,
        index_weight,
    )
    return query_grad.reshape(16, 64, 128), key_grad, weight_grad


def solution(mesh):
    placed = (
        P(None, "heads", None),
        P("keys", None),
        P("heads", None, None),
        P("keys", None),
        P("heads", None),
        P(),
        P("heads"),
    )
    return jax.shard_map(
        shards,
        mesh=mesh,
        in_specs=placed,
        out_specs=(P("heads", None, None), P("keys", None), P("heads", None)),
        check_vma=False,
    )
```

```python
import jax
import jax.numpy as jnp
from jax import lax
from jax.experimental import pallas as pl
from jax.experimental.pallas import tpu as pltpu
from jax.sharding import PartitionSpec as P

H = 128
SCALE = 192.0 ** (-0.5)
SCALE2 = SCALE * 1.4426950408889634
MASKED = -1e30
FLOOR = -1e29
MESH = pl.DeviceIdType.MESH
LAG = 3
NT = (((1,), (1,)), ((), ()))
F32 = jnp.float32
BF16 = jnp.bfloat16


def lanes(t):
    return slice(t * 128, (t + 1) * 128)


def fused(
    pos_s, kl_s, mqt_hbm, lkt_hbm, iq, ik, iw,
    qg_all, kg_all,
    mqt, lkt, mq_ref, posb_ref,
    s_a, s_b, e_ref, st_ref, stat_mine, stat_all,
    tp_ref, tc_ref, tx_ref, ty_ref,
    lg_ref, wpad_ref, wcol_ref, iqt_ref, is_ref, ie_ref, ist_mine, ist_all, d_ref,
    sl_ref, wgc_ref, qg_part, qg_recv, qg_xh,
    kp_ref, kc_ref, kx_ref, ky_ref,
    mq_in, lk_in,
    stat_ss, stat_rs, ist_ss, ist_rs,
    tc_ss, tc_rs, tx_ss, tx_rs, ty_ss, ty_rs,
    qg_ss, qg_rs, xh_ss, xh_rs, qa_ss, qa_rs,
    kc_ss, kc_rs, kx_ss, kx_rs, ky_ss, ky_rs, ka_ss, ka_rs,
):
    for i in range(8):
        pltpu.make_async_copy(mqt_hbm.at[i], mqt.at[i], mq_in.at[i]).start()
    pltpu.make_async_copy(lkt_hbm, lkt, lk_in).start()
    h = lax.axis_index("heads")
    k = lax.axis_index("keys")
    core, y, x = h % 2, (h // 2) % 4, h // 8
    z, xh = k // 2, k % 2
    key_first = k * 2048
    partner = x * 8 + y * 2 + (1 - core)
    across = (1 - x) * 8 + y * 2 + core

    def along_y(off):
        return x * 8 + ((y + off) % 4) * 2 + core

    def chip(b):
        return ((x + 1 - b // 4) % 2) * 4 + (y + 3 - b % 4) % 4

    barrier = pltpu.get_barrier_semaphore()
    for r in range(1, 16):
        pl.semaphore_signal(barrier, inc=1, device_id={"keys": (k + r) % 16}, device_id_type=MESH)
    for peer in (partner, across, along_y(1), along_y(2), along_y(3)):
        pl.semaphore_signal(barrier, inc=1, device_id={"heads": peer}, device_id_type=MESH)

    lane = lax.broadcasted_iota(jnp.int32, (1, 128), 1)
    sub = lax.broadcasted_iota(jnp.int32, (8, 128), 0)

    wpad_ref[...] = jnp.zeros((128, 128), F32)
    wpad_ref[0:16, 0:64] = iw[...]
    wturned = jnp.transpose(wpad_ref[...])
    for q in range(16):
        wcol_ref[q * 64:(q + 1) * 64, :] = jnp.broadcast_to(wturned[0:64, q:q + 1], (64, 128))
    for i in range(8):
        iqt_ref[:, lanes(i)] = jnp.transpose(iq[lanes(i), :].astype(F32) * wcol_ref[lanes(i), :]).astype(BF16)

    unit = lax.broadcasted_iota(jnp.int32, (256, 256), 0) == lax.broadcasted_iota(jnp.int32, (256, 256), 1)
    unit = jnp.where(unit, 1.0, 0.0).astype(BF16)

    def turn(i, carry):
        pltpu.make_async_copy(mqt_hbm.at[i], mqt.at[i], mq_in.at[i]).wait()
        got = lax.dot_general(unit, mqt[i], NT, preferred_element_type=F32).astype(BF16)
        for c in range(8):
            mq_ref[c, i] = got[c * 32:(c + 1) * 32, :]
        return carry

    lax.fori_loop(0, 8, turn, 0)
    pltpu.make_async_copy(lkt_hbm, lkt, lk_in).wait()

    def to_heads(src, dst, ss, rs, peer):
        return pltpu.make_async_remote_copy(
            src_ref=src, dst_ref=dst, send_sem=ss, recv_sem=rs,
            device_id={"heads": peer}, device_id_type=MESH,
        )

    def to_keys(src, dst, ss, rs, peer):
        return pltpu.make_async_remote_copy(
            src_ref=src, dst_ref=dst, send_sem=ss, recv_sem=rs,
            device_id={"keys": peer}, device_id_type=MESH,
        )

    def take(ref, sem):
        pltpu.make_async_copy(ref, ref, sem).wait()

    def score_quarter(b, i, s_ref):
        cols = pl.ds(pl.multiple_of(i * 512, 512), 512)
        s_ref[:, cols] = jnp.dot(
            mq_ref[chip(b)].reshape(256, 576), lkt[:, cols], preferred_element_type=F32
        )

    def soft_piece(b, i, s_ref):
        r0 = pl.multiple_of(chip(b) * 256, 256)
        rows = pl.ds(pl.multiple_of(i * 64, 64), 64)
        reach = jnp.concatenate([posb_ref[...]] * 2, axis=0)
        top = jnp.full((64, 128), FLOOR, F32)
        for t in range(16):
            v = jnp.where(reach >= t * 128, s_ref[rows, lanes(t)], MASKED)
            s_ref[rows, lanes(t)] = v
            top = jnp.maximum(top, v)
        mcol = jnp.broadcast_to(jnp.max(top, axis=1, keepdims=True), (64, 128))
        total = jnp.zeros((64, 128), F32)
        erows = pl.ds(pl.multiple_of(r0 + i * 64, 64), 64)
        for t in range(16):
            e = jnp.exp2((s_ref[rows, lanes(t)] - mcol) * SCALE2)
            total = total + e
            e_ref[erows, lanes(t)] = e.astype(BF16)
        lcol = jnp.broadcast_to(jnp.sum(total, axis=1, keepdims=True), (64, 128))
        st_ref[rows, :] = jnp.where(lane == 0, mcol, lcol)

    def reach_of(b):
        for n in range(4):
            got = jnp.zeros((8, 128), jnp.int32)
            for j in range(8):
                got = jnp.where(sub == j, pos_s[chip(b) * 32 + n * 8 + j] - key_first, got)
            posb_ref[n * 8:(n + 1) * 8, :] = got - lane

    def send_stats(b):
        stat_mine[b] = jnp.transpose(st_ref[...])[0:2, :]
        for r in range(1, 16):
            to_keys(stat_mine.at[b], stat_all.at[b, r - 1], stat_ss.at[b], stat_rs.at[b], (k + r) % 16).start()

    def target_block(b):
        take(stat_all.at[b], stat_rs.at[b])
        mine = stat_mine[b]
        m0, l0 = mine[0:1, :], mine[1:2, :]
        ms = [stat_all[b, r][0:1, :] for r in range(15)]
        ls = [stat_all[b, r][1:2, :] for r in range(15)]
        top = m0
        for m in ms:
            top = jnp.maximum(top, m)
        share = jnp.exp((m0 - top) * SCALE)
        total = l0 * share
        for m, l in zip(ms, ls):
            total = total + l * jnp.exp((m - top) * SCALE)
        w = share / (total * float(H))
        high = w.astype(BF16).astype(F32)
        low = w - high
        mine_of = lax.broadcasted_iota(jnp.int32, (32, 256), 1) % 32 == lax.broadcasted_iota(
            jnp.int32, (32, 256), 0
        )
        a = jnp.concatenate([jnp.where(mine_of, high, 0.0), jnp.where(mine_of, low, 0.0)], axis=0)
        r0 = pl.multiple_of(chip(b) * 256, 256)
        got = jnp.dot(a.astype(BF16), e_ref[pl.ds(r0, 256), :], preferred_element_type=F32)
        got = got[0:32, :] + got[32:64, :]
        tp_ref[b, 0] = got[0:16, :]
        tp_ref[b, 1] = got[16:32, :]
        to_heads(tp_ref.at[b, 1 - core], tc_ref.at[b], tc_ss.at[b], tc_rs.at[b], partner).start()

    def cross_x(b, p_ref, c_ref, x_ref, c_rs, x_ss, x_rs):
        take(c_ref.at[b], c_rs.at[b])
        p_ref[b, core] = p_ref[b, core] + c_ref[b]
        to_heads(p_ref.at[b, core], x_ref.at[b], x_ss.at[b], x_rs.at[b], across).start()

    def cross_y(i, p_ref, c_ref, x_ref, y_ref, c_rs, x_rs, y_ss, y_rs):
        b = 4 + i
        take(c_ref.at[b], c_rs.at[b])
        take(x_ref.at[i], x_rs.at[i])
        p_ref[b, core] = p_ref[b, core] + c_ref[b] + x_ref[i]
        off = 3 - i
        if off:
            to_heads(
                p_ref.at[b, core], y_ref.at[off - 1], y_ss.at[off - 1], y_rs.at[off - 1], along_y(off)
            ).start()

    def first(i, carry):
        score_quarter(0, i, s_a)
        return carry

    lax.fori_loop(0, 4, first, 0)
    pl.semaphore_wait(barrier, 20)

    def one_block(b, s_now, s_next):
        reach_of(b)

        def quarter(i, carry):
            score_quarter(jnp.minimum(b + 1, 7), i, s_next)
            soft_piece(b, i, s_now)
            return carry

        lax.fori_loop(0, 4, quarter, 0)
        send_stats(b)

        @pl.when(b >= LAG)
        def _():
            target_block(b - LAG)

        @pl.when(b >= LAG + 1)
        def _():
            cross_x(b - LAG - 1, tp_ref, tc_ref, tx_ref, tc_rs, tx_ss, tx_rs)

    def two_blocks(n, carry):
        one_block(n * 2, s_a, s_b)
        one_block(n * 2 + 1, s_b, s_a)
        return carry

    lax.fori_loop(0, 4, two_blocks, 0)

    def index_step(g, carry):
        rows = pl.ds(pl.multiple_of(g * 256, 256), 256)

        def quarter(i, inner):
            got = lax.dot_general(
                iq[rows, :], ik[pl.ds(pl.multiple_of(i * 512, 512), 512), :], NT, preferred_element_type=F32
            )
            for t in range(4):
                cols = pl.ds(pl.multiple_of(i * 512 + t * 128, 128), 128)
                for j in range(4):
                    qrows = pl.ds(pl.multiple_of(g * 256 + j * 64, 64), 64)
                    v = got[j * 64:(j + 1) * 64, lanes(t)]
                    lg_ref[qrows, cols] = v.astype(BF16)
                    is_ref[g, j:j + 1, cols] = jnp.sum(
                        jnp.maximum(v, 0.0) * wcol_ref[qrows, :], axis=0, keepdims=True
                    )
            return inner

        lax.fori_loop(0, 4, quarter, 0)

        @pl.when(g < LAG)
        def _():
            target_block(8 - LAG + g)

        return carry

    lax.fori_loop(0, 4, index_step, 0)

    row = lax.broadcasted_iota(jnp.int32, (16, 128), 0)
    posr = jnp.zeros((16, 128), jnp.int32)
    klr = jnp.zeros((16, 128), F32)
    for q in range(16):
        posr = jnp.where(row == q, pos_s[h * 16 + q] - key_first, posr)
        klr = jnp.where(row == q, kl_s[q], klr)
    top = jnp.full((16, 128), FLOOR, F32)
    for t in range(16):
        v = jnp.concatenate([is_ref[g, 0:4, lanes(t)] for g in range(4)], axis=0)
        v = jnp.where(lane + t * 128 <= posr, v, MASKED)
        ie_ref[:, lanes(t)] = v
        top = jnp.maximum(top, v)
    im = jnp.broadcast_to(jnp.max(top, axis=1, keepdims=True), (16, 128))
    total = jnp.zeros((16, 128), F32)
    for t in range(16):
        e = jnp.exp(ie_ref[:, lanes(t)] - im)
        total = total + e
        ie_ref[:, lanes(t)] = e
    il = jnp.broadcast_to(jnp.sum(total, axis=1, keepdims=True), (16, 128))
    ist_mine[...] = jnp.where(lane == 0, im, il)
    for r in range(1, 16):
        to_keys(ist_mine, ist_all.at[r - 1], ist_ss, ist_rs, (k + r) % 16).start()

    for i in range(4):
        cross_y(i, tp_ref, tc_ref, tx_ref, ty_ref, tc_rs, tx_rs, ty_ss, ty_rs)

    take(ist_all, ist_rs)
    ms = [jnp.broadcast_to(ist_all[r][:, 0:1], (16, 128)) for r in range(15)]
    top = im
    for m in ms:
        top = jnp.maximum(top, m)
    share = jnp.exp(im - top)
    total = il * share
    for r in range(15):
        total = total + jnp.broadcast_to(ist_all[r][:, 1:2], (16, 128)) * jnp.exp(ms[r] - top)
    share = share / total

    for j in range(3):
        take(ty_ref.at[j], ty_rs.at[j])
    for t in range(16):
        target = tp_ref[7, core, :, lanes(t)]
        for j in range(3):
            target = target + ty_ref[j, :, lanes(t)]
        delta = klr * (ie_ref[:, lanes(t)] * share - target)
        for q in range(16):
            d_ref[q, :, lanes(t)] = jnp.broadcast_to(delta[q:q + 1, :], (16, 128)).astype(BF16)

    def back_step(n, carry):
        g = (z // 2 + 1 + n) % 4
        rows = pl.ds(pl.multiple_of(g * 256, 256), 256)
        for j in range(4):
            qrows = pl.ds(pl.multiple_of(g * 256 + j * 64, 64), 64)
            for t in range(16):
                d = jnp.concatenate([d_ref[g * 4 + j, :, lanes(t)]] * 4, axis=0)
                sl_ref[qrows, lanes(t)] = jnp.where(lg_ref[qrows, lanes(t)] > 0, d, jnp.zeros((64, 128), BF16))
        got = jnp.dot(sl_ref[rows, :], ik[...], preferred_element_type=F32)
        along = jnp.sum(got * iq[rows, :].astype(F32), axis=1, keepdims=True)
        wgc_ref[...] = jnp.zeros((128, 128), F32)
        columns = jnp.zeros((64, 128), F32)
        for j in range(4):
            at = (j // 2) * 8 + j % 2
            columns = jnp.where(lane == at, jnp.broadcast_to(along[j * 64:(j + 1) * 64], (64, 128)), columns)
        wgc_ref[0:64, :] = columns
        turned = jnp.transpose(wgc_ref[...])
        got = got * wcol_ref[rows, :]
        for j in range(2):
            blk = g * 2 + j
            qg_part[blk, 0:128, :] = got[j * 128:(j + 1) * 128, :]
            qg_part[blk, 128:136, :] = turned[j * 8:(j + 1) * 8, :]
            r = (blk - z + 8) % 8

            @pl.when(r > 0)
            def _():
                to_keys(
                    qg_part.at[blk], qg_recv.at[r - 1], qg_ss.at[r - 1], qg_rs.at[r - 1], blk * 2 + xh
                ).start()

        return carry

    lax.fori_loop(0, 4, back_step, 0)

    def key_step(b, carry):
        cols = pl.ds(pl.multiple_of(chip(b) * 256, 256), 256)
        got = jnp.dot(iqt_ref[...], sl_ref[:, cols], preferred_element_type=F32)
        kp_ref[b, 0] = got[:, 0:128]
        kp_ref[b, 1] = got[:, 128:256]
        to_heads(kp_ref.at[b, 1 - core], kc_ref.at[b], kc_ss.at[b], kc_rs.at[b], partner).start()

        @pl.when((b >= 1) & (b < 5))
        def _():
            cross_x(b - 1, kp_ref, kc_ref, kx_ref, kc_rs, kx_ss, kx_rs)

        return carry

    lax.fori_loop(0, 8, key_step, 0)

    for j in range(7):
        take(qg_recv.at[j], qg_rs.at[j])
    acc = qg_part[z]
    for j in range(7):
        acc = acc + qg_recv[j]
    qg_part[z] = acc
    to_keys(qg_part.at[z], qg_xh, xh_ss, xh_rs, z * 2 + (1 - xh)).start()

    for i in range(4):
        cross_y(i, kp_ref, kc_ref, kx_ref, ky_ref, kc_rs, kx_rs, ky_ss, ky_rs)

    take(qg_xh, xh_rs)
    qg_all[z] = qg_part[z] + qg_xh[...]
    for r in range(1, 8):
        to_keys(
            qg_all.at[z], qg_all.at[z], qa_ss.at[r - 1], qa_rs.at[r - 1], ((z + r) % 8) * 2 + xh
        ).start()

    for j in range(3):
        take(ky_ref.at[j], ky_rs.at[j])
    shard = kp_ref[7, core]
    for j in range(3):
        shard = shard + ky_ref[j]
    kg_all[h] = jnp.transpose(shard)

    def pass_on(s, peer, n):
        to_heads(kg_all.at[s], kg_all.at[s], ka_ss.at[n], ka_rs.at[s], peer).start()

    for off in (1, 2, 3):
        pass_on(h, along_y(off), off - 1)
    pass_on(h, across, 3)
    pass_on(h, partner, 4)
    for off in (1, 3, 2):
        s = along_y(off)
        take(kg_all.at[s], ka_rs.at[s])
        pass_on(s, across, 4 + off)
        pass_on(s, partner, 7 + off)
    for off in (0, 1, 3, 2):
        s = (1 - x) * 8 + ((y + off) % 4) * 2 + core
        take(kg_all.at[s], ka_rs.at[s])
        pass_on(s, partner, 11 + off)

    for r in range(1, 8):
        take(qg_all.at[(z - r + 8) % 8], qa_rs.at[r - 1])
    for c in range(8):
        s = c * 2 + (1 - core)
        take(kg_all.at[s], ka_rs.at[s])

    for b in range(8):
        take(stat_all.at[b], stat_ss.at[b])
        take(tc_ref.at[b], tc_ss.at[b])
        take(kc_ref.at[b], kc_ss.at[b])
    take(ist_all, ist_ss)
    for b in range(4):
        take(tx_ref.at[b], tx_ss.at[b])
        take(kx_ref.at[b], kx_ss.at[b])
    for j in range(3):
        take(ty_ref.at[j], ty_ss.at[j])
        take(ky_ref.at[j], ky_ss.at[j])
    for j in range(7):
        take(qg_recv.at[j], qg_ss.at[j])
        take(qg_all.at[j], qa_ss.at[j])
    take(qg_xh, xh_ss)
    for n in range(15):
        take(kg_all.at[n], ka_ss.at[n])


def finish(qg_all, kg_all, qg_out, kg_out, wg_out):
    for i in range(8):
        qg_out[i * 128:(i + 1) * 128, :] = qg_all[i, 0:128, :]
        wg_out[i * 2:(i + 1) * 2, :] = qg_all[i, 128:130, 0:64]
    for i in range(16):
        kg_out[i * 128:(i + 1) * 128, :] = kg_all[i]


def shards(main_query, latent_keys, index_query, index_keys, index_weight, query_pos, kl_weight):
    vmem = pl.BlockSpec(memory_space=pltpu.VMEM)
    smem = pl.BlockSpec(memory_space=pltpu.SMEM)
    hbm = pl.BlockSpec(memory_space=pl.ANY)
    dma = pltpu.SemaphoreType.DMA
    query_blocks, key_blocks = pl.pallas_call(
        fused,
        out_shape=(
            jax.ShapeDtypeStruct((8, 136, 128), F32),
            jax.ShapeDtypeStruct((16, 128, 128), F32),
        ),
        in_specs=[smem, smem, hbm, hbm, vmem, vmem, vmem],
        out_specs=(vmem, vmem),
        scratch_shapes=[
            pltpu.VMEM((8, 576, 256), BF16),
            pltpu.VMEM((576, 2048), BF16),
            pltpu.VMEM((8, 8, 32, 576), BF16),
            pltpu.VMEM((32, 128), jnp.int32),
            pltpu.VMEM((256, 2048), F32),
            pltpu.VMEM((256, 2048), F32),
            pltpu.VMEM((2048, 2048), BF16),
            pltpu.VMEM((256, 128), F32),
            pltpu.VMEM((8, 2, 256), F32),
            pltpu.VMEM((8, 15, 2, 256), F32),
            pltpu.VMEM((8, 2, 16, 2048), F32),
            pltpu.VMEM((8, 16, 2048), F32),
            pltpu.VMEM((4, 16, 2048), F32),
            pltpu.VMEM((3, 16, 2048), F32),
            pltpu.VMEM((1024, 2048), BF16),
            pltpu.VMEM((128, 128), F32),
            pltpu.VMEM((1024, 128), F32),
            pltpu.VMEM((128, 1024), BF16),
            pltpu.VMEM((4, 8, 2048), F32),
            pltpu.VMEM((16, 2048), F32),
            pltpu.VMEM((16, 128), F32),
            pltpu.VMEM((15, 16, 128), F32),
            pltpu.VMEM((16, 16, 2048), BF16),
            pltpu.VMEM((1024, 2048), BF16),
            pltpu.VMEM((128, 128), F32),
            pltpu.VMEM((8, 136, 128), F32),
            pltpu.VMEM((7, 136, 128), F32),
            pltpu.VMEM((136, 128), F32),
            pltpu.VMEM((8, 2, 128, 128), F32),
            pltpu.VMEM((8, 128, 128), F32),
            pltpu.VMEM((4, 128, 128), F32),
            pltpu.VMEM((3, 128, 128), F32),
            dma((8,)), dma,
            dma((8,)), dma((8,)), dma, dma,
            dma((8,)), dma((8,)), dma((4,)), dma((4,)), dma((3,)), dma((3,)),
            dma((7,)), dma((7,)), dma, dma, dma((7,)), dma((7,)),
            dma((8,)), dma((8,)), dma((4,)), dma((4,)), dma((3,)), dma((3,)),
            dma((15,)), dma((16,)),
        ],
        compiler_params=pltpu.CompilerParams(
            collective_id=0, has_side_effects=True, vmem_limit_bytes=60 * 1024 * 1024
        ),
        name="fused_indexer_step",
    )(
        query_pos,
        kl_weight,
        jnp.transpose(main_query, (1, 2, 0)),
        jnp.transpose(latent_keys, (1, 0)),
        index_query.reshape(1024, 128),
        index_keys,
        index_weight,
    )
    query_grad, key_grad, weight_grad = pl.pallas_call(
        finish,
        out_shape=(
            jax.ShapeDtypeStruct((1024, 128), F32),
            jax.ShapeDtypeStruct((2048, 128), F32),
            jax.ShapeDtypeStruct((16, 64), F32),
        ),
        in_specs=[vmem, vmem],
        out_specs=(vmem, vmem, vmem),
        name="finish",
    )(query_blocks, key_blocks)
    return query_grad.reshape(16, 64, 128), key_grad, weight_grad


def solution(mesh):
    placed = (
        P(None, "heads", None),
        P("keys", None),
        P("heads", None, None),
        P("keys", None),
        P("heads", None),
        P(),
        P("heads"),
    )
    return jax.shard_map(
        shards,
        mesh=mesh,
        in_specs=placed,
        out_specs=(P("heads", None, None), P("keys", None), P("heads", None)),
        check_vma=False,
    )
```

```python
import functools

import jax
import jax.numpy as jnp
from jax import lax
from jax.experimental import pallas as pl
from jax.experimental.pallas import tpu as pltpu
from jax.sharding import PartitionSpec as P

H = 128
SCALE = 192.0 ** (-0.5)
SCALE2 = SCALE * 1.4426950408889634
MASKED = -1e30
FLOOR = -1e29
MESH = pl.DeviceIdType.MESH
LAG = 3
NT = (((1,), (1,)), ((), ()))
F32 = jnp.float32
BF16 = jnp.bfloat16


def lanes(t):
    return slice(t * 128, (t + 1) * 128)


def fused(
    pos_s, kl_s, mqt_hbm, lkt_hbm, iq, ik, iw,
    qg_all, kg_all,
    mqt, lkt_in, posb_ref,
    s_a, s_b, st_ref, stat_mine, stat_all,
    tp_ref, tc_ref, tx_ref, ty_ref,
    wpad_ref, wcol_ref, is_ref, ie_ref, ist_mine, ist_all,
    wgc_ref, qg_part, qg_recv, qg_four, qg_xh,
    kp_ref, kc_ref, kx_ref, ky_ref,
    mq_in, lk_in,
    stat_ss, stat_rs, ist_ss, ist_rs,
    tc_ss, tc_rs, tx_ss, tx_rs, ty_ss, ty_rs,
    qg_ss, qg_rs, xh_ss, xh_rs, qa_ss, qa_rs,
    kc_ss, kc_rs, kx_ss, kx_rs, ky_ss, ky_rs, ka_ss, ka_rs,
    lkt, mq_ref, e_ref, lg_ref, iqt_ref, ikc, d_ref, sl_ref,
):
    for i in range(8):
        pltpu.make_async_copy(mqt_hbm.at[i], mqt.at[i], mq_in.at[i]).start()
    pltpu.make_async_copy(lkt_hbm, lkt_in, lk_in).start()
    h = lax.axis_index("heads")
    k = lax.axis_index("keys")
    core, y, x = h % 2, (h // 2) % 4, h // 8
    z, xh = k // 2, k % 2
    key_first = k * 2048
    partner = x * 8 + y * 2 + (1 - core)
    across = (1 - x) * 8 + y * 2 + core

    def along_y(off):
        return x * 8 + ((y + off) % 4) * 2 + core

    def chip(b):
        return ((x + 1 - b // 4) % 2) * 4 + (y + 3 - b % 4) % 4

    barrier = pltpu.get_barrier_semaphore()
    for r in range(1, 16):
        pl.semaphore_signal(barrier, inc=1, device_id={"keys": (k + r) % 16}, device_id_type=MESH)
    for peer in (partner, across, along_y(1), along_y(2), along_y(3)):
        pl.semaphore_signal(barrier, inc=1, device_id={"heads": peer}, device_id_type=MESH)

    lane = lax.broadcasted_iota(jnp.int32, (1, 128), 1)
    sub = lax.broadcasted_iota(jnp.int32, (8, 128), 0)

    unit = lax.broadcasted_iota(jnp.int32, (256, 256), 0) == lax.broadcasted_iota(jnp.int32, (256, 256), 1)
    unit = jnp.where(unit, 1.0, 0.0).astype(BF16)

    def turn(i, carry):
        pltpu.make_async_copy(mqt_hbm.at[i], mqt.at[i], mq_in.at[i]).wait()
        got = lax.dot_general(unit, mqt[i], NT, preferred_element_type=F32).astype(BF16)
        for c in range(8):
            mq_ref[c, i] = got[c * 32:(c + 1) * 32, :]
        return carry

    lax.fori_loop(0, 8, turn, 0)
    pltpu.make_async_copy(lkt_hbm, lkt_in, lk_in).wait()

    def settle(i, carry):
        rows = pl.ds(pl.multiple_of(i * 64, 64), 64)
        lkt[rows, :] = lkt_in[rows, :]
        return carry

    lax.fori_loop(0, 9, settle, 0)
    ikc[...] = ik[...]

    def to_heads(src, dst, ss, rs, peer):
        return pltpu.make_async_remote_copy(
            src_ref=src, dst_ref=dst, send_sem=ss, recv_sem=rs,
            device_id={"heads": peer}, device_id_type=MESH,
        )

    def to_keys(src, dst, ss, rs, peer):
        return pltpu.make_async_remote_copy(
            src_ref=src, dst_ref=dst, send_sem=ss, recv_sem=rs,
            device_id={"keys": peer}, device_id_type=MESH,
        )

    def take(ref, sem):
        pltpu.make_async_copy(ref, ref, sem).wait()

    def score_quarter(b, i, s_ref):
        cols = pl.ds(pl.multiple_of(i * 512, 512), 512)
        s_ref[:, cols] = jnp.dot(
            mq_ref[chip(b)].reshape(256, 576), lkt[:, cols], preferred_element_type=F32
        )

    def soft_piece(b, i, s_ref):
        r0 = pl.multiple_of(chip(b) * 256, 256)
        rows = pl.ds(pl.multiple_of(i * 64, 64), 64)
        reach = jnp.concatenate([posb_ref[...]] * 2, axis=0)
        top = jnp.full((64, 128), FLOOR, F32)
        for t in range(16):
            v = jnp.where(reach >= t * 128, s_ref[rows, lanes(t)], MASKED)
            s_ref[rows, lanes(t)] = v
            top = jnp.maximum(top, v)
        mcol = jnp.broadcast_to(jnp.max(top, axis=1, keepdims=True), (64, 128))
        total = jnp.zeros((64, 128), F32)
        erows = pl.ds(pl.multiple_of(r0 + i * 64, 64), 64)
        for t in range(16):
            e = jnp.exp2((s_ref[rows, lanes(t)] - mcol) * SCALE2)
            total = total + e
            e_ref[erows, lanes(t)] = e.astype(BF16)
        lcol = jnp.broadcast_to(jnp.sum(total, axis=1, keepdims=True), (64, 128))
        st_ref[rows, :] = jnp.where(lane == 0, mcol, lcol)

    def reach_of(b):
        for n in range(4):
            got = jnp.zeros((8, 128), jnp.int32)
            for j in range(8):
                got = jnp.where(sub == j, pos_s[chip(b) * 32 + n * 8 + j] - key_first, got)
            posb_ref[n * 8:(n + 1) * 8, :] = got - lane

    def send_stats(b):
        stat_mine[b] = jnp.transpose(st_ref[...])[0:2, :]
        for r in range(1, 16):
            to_keys(stat_mine.at[b], stat_all.at[b, r - 1], stat_ss.at[b], stat_rs.at[b], (k + r) % 16).start()

    def target_block(b):
        take(stat_all.at[b], stat_rs.at[b])
        mine = stat_mine[b]
        m0, l0 = mine[0:1, :], mine[1:2, :]
        ms = [stat_all[b, r][0:1, :] for r in range(15)]
        ls = [stat_all[b, r][1:2, :] for r in range(15)]
        top = m0
        for m in ms:
            top = jnp.maximum(top, m)
        share = jnp.exp((m0 - top) * SCALE)
        total = l0 * share
        for m, l in zip(ms, ls):
            total = total + l * jnp.exp((m - top) * SCALE)
        w = share / (total * float(H))
        high = w.astype(BF16).astype(F32)
        low = w - high
        mine_of = lax.broadcasted_iota(jnp.int32, (32, 256), 1) % 32 == lax.broadcasted_iota(
            jnp.int32, (32, 256), 0
        )
        a = jnp.concatenate([jnp.where(mine_of, high, 0.0), jnp.where(mine_of, low, 0.0)], axis=0)
        r0 = pl.multiple_of(chip(b) * 256, 256)
        got = jnp.dot(a.astype(BF16), e_ref[pl.ds(r0, 256), :], preferred_element_type=F32)
        got = got[0:32, :] + got[32:64, :]
        tp_ref[b, 0] = got[0:16, :]
        tp_ref[b, 1] = got[16:32, :]
        to_heads(tp_ref.at[b, 1 - core], tc_ref.at[b], tc_ss.at[b], tc_rs.at[b], partner).start()

    def cross_x(b, p_ref, c_ref, x_ref, c_rs, x_ss, x_rs):
        take(c_ref.at[b], c_rs.at[b])
        p_ref[b, core] = p_ref[b, core] + c_ref[b]
        to_heads(p_ref.at[b, core], x_ref.at[b], x_ss.at[b], x_rs.at[b], across).start()

    def cross_y(i, p_ref, c_ref, x_ref, y_ref, c_rs, x_rs, y_ss, y_rs):
        b = 4 + i
        take(c_ref.at[b], c_rs.at[b])
        take(x_ref.at[i], x_rs.at[i])
        p_ref[b, core] = p_ref[b, core] + c_ref[b] + x_ref[i]
        off = 3 - i
        if off:
            to_heads(
                p_ref.at[b, core], y_ref.at[off - 1], y_ss.at[off - 1], y_rs.at[off - 1], along_y(off)
            ).start()

    def first(i, carry):
        score_quarter(0, i, s_a)
        return carry

    lax.fori_loop(0, 4, first, 0)
    pl.semaphore_wait(barrier, 20)

    def one_block(b, s_now, s_next):
        reach_of(b)

        for i in range(4):
            score_quarter(jnp.minimum(b + 1, 7), i, s_next)
            soft_piece(b, i, s_now)
        send_stats(b)

        @pl.when(b >= LAG)
        def _():
            target_block(b - LAG)

        @pl.when(b >= LAG + 1)
        def _():
            cross_x(b - LAG - 1, tp_ref, tc_ref, tx_ref, tc_rs, tx_ss, tx_rs)

    def two_blocks(n, carry):
        one_block(n * 2, s_a, s_b)
        one_block(n * 2 + 1, s_b, s_a)
        return carry

    lax.fori_loop(0, 4, two_blocks, 0)

    wpad_ref[...] = jnp.zeros((128, 128), F32)
    wpad_ref[0:16, 0:64] = iw[...]
    wturned = jnp.transpose(wpad_ref[...])
    for q in range(16):
        wcol_ref[q * 64:(q + 1) * 64, :] = jnp.broadcast_to(wturned[0:64, q:q + 1], (64, 128))
    for i in range(8):
        iqt_ref[:, lanes(i)] = jnp.transpose(iq[lanes(i), :].astype(F32) * wcol_ref[lanes(i), :]).astype(BF16)

    def index_step(g, carry):
        rows = pl.ds(pl.multiple_of(g * 256, 256), 256)

        def part(i, inner):
            got = lax.dot_general(
                iq[rows, :], ikc[pl.ds(pl.multiple_of(i * 256, 256), 256), :], NT, preferred_element_type=F32
            )
            for j in range(4):
                qrows = pl.ds(pl.multiple_of(g * 256 + j * 64, 64), 64)
                for t in range(2):
                    cols = pl.ds(pl.multiple_of(i * 256 + t * 128, 128), 128)
                    v = got[j * 64:(j + 1) * 64, lanes(t)]
                    lg_ref[qrows, cols] = v.astype(BF16)
                    is_ref[g, j:j + 1, cols] = jnp.sum(
                        jnp.maximum(v, 0.0) * wcol_ref[qrows, :], axis=0, keepdims=True
                    )
            return inner

        lax.fori_loop(0, 8, part, 0)

        @pl.when(g < LAG)
        def _():
            target_block(8 - LAG + g)

        return carry

    lax.fori_loop(0, 4, index_step, 0)

    row = lax.broadcasted_iota(jnp.int32, (16, 128), 0)
    posr = jnp.zeros((16, 128), jnp.int32)
    klr = jnp.zeros((16, 128), F32)
    for q in range(16):
        posr = jnp.where(row == q, pos_s[h * 16 + q] - key_first, posr)
        klr = jnp.where(row == q, kl_s[q], klr)
    top = jnp.full((16, 128), FLOOR, F32)
    for t in range(16):
        v = jnp.concatenate([is_ref[g, 0:4, lanes(t)] for g in range(4)], axis=0)
        v = jnp.where(lane + t * 128 <= posr, v, MASKED)
        ie_ref[:, lanes(t)] = v
        top = jnp.maximum(top, v)
    im = jnp.broadcast_to(jnp.max(top, axis=1, keepdims=True), (16, 128))
    total = jnp.zeros((16, 128), F32)
    for t in range(16):
        e = jnp.exp(ie_ref[:, lanes(t)] - im)
        total = total + e
        ie_ref[:, lanes(t)] = e
    il = jnp.broadcast_to(jnp.sum(total, axis=1, keepdims=True), (16, 128))
    ist_mine[...] = jnp.where(lane == 0, im, il)
    for r in range(1, 16):
        to_keys(ist_mine, ist_all.at[r - 1], ist_ss, ist_rs, (k + r) % 16).start()

    for i in range(4):
        cross_y(i, tp_ref, tc_ref, tx_ref, ty_ref, tc_rs, tx_rs, ty_ss, ty_rs)

    take(ist_all, ist_rs)
    ms = [jnp.broadcast_to(ist_all[r][:, 0:1], (16, 128)) for r in range(15)]
    top = im
    for m in ms:
        top = jnp.maximum(top, m)
    share = jnp.exp(im - top)
    total = il * share
    for r in range(15):
        total = total + jnp.broadcast_to(ist_all[r][:, 1:2], (16, 128)) * jnp.exp(ms[r] - top)
    share = share / total

    for j in range(3):
        take(ty_ref.at[j], ty_rs.at[j])
    for t in range(16):
        target = tp_ref[7, core, :, lanes(t)]
        for j in range(3):
            target = target + ty_ref[j, :, lanes(t)]
        delta = klr * (ie_ref[:, lanes(t)] * share - target)
        for q in range(16):
            d_ref[q, :, lanes(t)] = jnp.broadcast_to(delta[q:q + 1, :], (16, 128)).astype(BF16)

    def z_peer(off):
        return ((z + off) % 8) * 2 + xh

    def back_step(offsets):
        picked = []
        for off in offsets:
            q0 = ((z + off) % 8) * 2
            for j in range(2):
                qrows = pl.ds(pl.multiple_of((q0 + j) * 64, 64), 64)
                for t in range(16):
                    d = jnp.concatenate([d_ref[q0 + j, :, lanes(t)]] * 4, axis=0)
                    sl_ref[qrows, lanes(t)] = jnp.where(
                        lg_ref[qrows, lanes(t)] > 0, d, jnp.zeros((64, 128), BF16)
                    )
            picked.append(pl.ds(pl.multiple_of(q0 * 64, 128), 128))
        gate = jnp.concatenate([sl_ref[rows, :] for rows in picked], axis=0)
        both = jnp.dot(gate, ikc[...], preferred_element_type=F32)
        columns = jnp.zeros((64, 128), F32)
        for n, (off, rows) in enumerate(zip(offsets, picked)):
            got = both[n * 128:(n + 1) * 128, :]
            along = jnp.sum(got * iq[rows, :].astype(F32), axis=1, keepdims=True)
            for j in range(2):
                columns = jnp.where(
                    lane == n * 8 + j, jnp.broadcast_to(along[j * 64:(j + 1) * 64], (64, 128)), columns
                )
            qg_part[off, 0:128, :] = got * wcol_ref[rows, :]
        wgc_ref[0:64, :] = columns
        turned = jnp.transpose(wgc_ref[...])
        for n, off in enumerate(offsets):
            qg_part[off, 128:136, :] = turned[n * 8:(n + 1) * 8, :]

    def z_send(src, dst, n, off):
        to_keys(src, dst, qg_ss.at[n], qg_rs.at[n], z_peer(off)).start()

    wgc_ref[...] = jnp.zeros((128, 128), F32)
    back_step((4, 3))
    z_send(qg_part.at[4, 0:72], qg_four.at[0:72], 0, 2)
    z_send(qg_part.at[4, 72:136], qg_four.at[72:136], 1, 6)
    z_send(qg_part.at[3], qg_recv.at[0], 2, 1)
    back_step((5, 2))
    z_send(qg_part.at[5], qg_recv.at[1], 3, 7)
    back_step((6, 1))
    z_send(qg_part.at[1], qg_recv.at[2], 4, 1)
    back_step((7, 0))
    z_send(qg_part.at[7], qg_recv.at[3], 5, 7)

    def z_join():
        take(qg_recv.at[0], qg_rs.at[2])
        take(qg_four.at[0:72], qg_rs.at[0])
        qg_part[2, 0:72, :] = qg_part[2, 0:72, :] + qg_recv[0, 0:72, :] + qg_four[0:72, :]
        qg_part[2, 72:136, :] = qg_part[2, 72:136, :] + qg_recv[0, 72:136, :]
        z_send(qg_part.at[2], qg_recv.at[4], 6, 2)
        take(qg_recv.at[1], qg_rs.at[3])
        take(qg_four.at[72:136], qg_rs.at[1])
        qg_part[6, 0:72, :] = qg_part[6, 0:72, :] + qg_recv[1, 0:72, :]
        qg_part[6, 72:136, :] = qg_part[6, 72:136, :] + qg_recv[1, 72:136, :] + qg_four[72:136, :]
        z_send(qg_part.at[6], qg_recv.at[5], 7, 6)

    def key_step(b, carry):
        cols = pl.ds(pl.multiple_of(chip(b) * 256, 256), 256)
        got = jnp.dot(iqt_ref[...], sl_ref[:, cols], preferred_element_type=F32)
        kp_ref[b, 0] = got[:, 0:128]
        kp_ref[b, 1] = got[:, 128:256]
        to_heads(kp_ref.at[b, 1 - core], kc_ref.at[b], kc_ss.at[b], kc_rs.at[b], partner).start()

        @pl.when(b == 2)
        def _():
            z_join()

        @pl.when((b >= 1) & (b < 5))
        def _():
            cross_x(b - 1, kp_ref, kc_ref, kx_ref, kc_rs, kx_ss, kx_rs)

        return carry

    lax.fori_loop(0, 8, key_step, 0)

    for i in range(4):
        cross_y(i, kp_ref, kc_ref, kx_ref, ky_ref, kc_rs, kx_rs, ky_ss, ky_rs)

    for j in range(4):
        take(qg_recv.at[2 + j], qg_rs.at[4 + j])
    qg_part[0] = qg_part[0] + (qg_recv[2] + qg_recv[3]) + (qg_recv[4] + qg_recv[5])
    to_keys(qg_part.at[0], qg_xh, xh_ss, xh_rs, z * 2 + (1 - xh)).start()

    for j in range(3):
        take(ky_ref.at[j], ky_rs.at[j])
    shard = kp_ref[7, core]
    for j in range(3):
        shard = shard + ky_ref[j]
    kg_all[h] = jnp.transpose(shard)

    def pass_on(s, peer, n):
        to_heads(kg_all.at[s], kg_all.at[s], ka_ss.at[n], ka_rs.at[s], peer).start()

    for off in (1, 2, 3):
        pass_on(h, along_y(off), off - 1)
    pass_on(h, across, 3)
    pass_on(h, partner, 4)

    def z_back(off_from, part, n, off):
        ref = qg_all.at[(z + off_from) % 8, part]
        to_keys(ref, ref, qa_ss.at[n], qa_rs.at[n], z_peer(off)).start()

    def z_take(off_from, part, n):
        take(qg_all.at[(z + off_from) % 8, part], qa_rs.at[n])

    whole, front, rear = slice(0, 136), slice(0, 72), slice(72, 136)
    take(qg_xh, xh_rs)
    qg_all[z] = qg_part[0] + qg_xh[...]
    z_back(0, whole, 0, 2)
    z_back(0, whole, 1, 6)
    z_back(0, whole, 2, 1)
    z_back(0, whole, 3, 7)
    for off in (1, 3, 2):
        s = along_y(off)
        take(kg_all.at[s], ka_rs.at[s])
        pass_on(s, across, 4 + off)
        pass_on(s, partner, 7 + off)
    z_take(6, whole, 0)
    z_back(6, front, 4, 2)
    z_back(6, whole, 5, 1)
    z_take(2, whole, 1)
    z_back(2, rear, 6, 6)
    z_back(2, whole, 7, 7)
    for off in (0, 1, 3, 2):
        s = (1 - x) * 8 + ((y + off) % 4) * 2 + core
        take(kg_all.at[s], ka_rs.at[s])
        pass_on(s, partner, 11 + off)

    z_take(7, whole, 2)
    z_take(1, whole, 3)
    z_take(4, front, 4)
    z_take(5, whole, 5)
    z_take(4, rear, 6)
    z_take(3, whole, 7)
    for c in range(8):
        s = c * 2 + (1 - core)
        take(kg_all.at[s], ka_rs.at[s])

    for b in range(8):
        take(stat_all.at[b], stat_ss.at[b])
        take(tc_ref.at[b], tc_ss.at[b])
        take(kc_ref.at[b], kc_ss.at[b])
    take(ist_all, ist_ss)
    for b in range(4):
        take(tx_ref.at[b], tx_ss.at[b])
        take(kx_ref.at[b], kx_ss.at[b])
    for j in range(3):
        take(ty_ref.at[j], ty_ss.at[j])
        take(ky_ref.at[j], ky_ss.at[j])
    take(qg_four.at[0:72], qg_ss.at[0])
    take(qg_four.at[72:136], qg_ss.at[1])
    for j in range(6):
        take(qg_recv.at[j], qg_ss.at[2 + j])
    for n, part in enumerate((whole, whole, whole, whole, front, whole, rear, whole)):
        take(qg_all.at[0, part], qa_ss.at[n])
    take(qg_xh, xh_ss)
    for n in range(15):
        take(kg_all.at[n], ka_ss.at[n])


def scoped(*refs):
    pl.run_scoped(
        functools.partial(fused, *refs),
        pltpu.VMEM((576, 2048), BF16),
        pltpu.VMEM((8, 8, 32, 576), BF16),
        pltpu.VMEM((2048, 2048), BF16),
        pltpu.VMEM((1024, 2048), BF16),
        pltpu.VMEM((128, 1024), BF16),
        pltpu.VMEM((2048, 128), BF16),
        pltpu.VMEM((16, 16, 2048), BF16),
        pltpu.VMEM((1024, 2048), BF16),
    )


def finish(qg_all, kg_all, qg_out, kg_out, wg_out):
    for i in range(8):
        qg_out[i * 128:(i + 1) * 128, :] = qg_all[i, 0:128, :]
        wg_out[i * 2:(i + 1) * 2, :] = qg_all[i, 128:130, 0:64]
    for i in range(16):
        kg_out[i * 128:(i + 1) * 128, :] = kg_all[i]


def shards(main_query, latent_keys, index_query, index_keys, index_weight, query_pos, kl_weight):
    vmem = pl.BlockSpec(memory_space=pltpu.VMEM)
    smem = pl.BlockSpec(memory_space=pltpu.SMEM)
    hbm = pl.BlockSpec(memory_space=pl.ANY)
    dma = pltpu.SemaphoreType.DMA
    query_blocks, key_blocks = pl.pallas_call(
        scoped,
        out_shape=(
            jax.ShapeDtypeStruct((8, 136, 128), F32),
            jax.ShapeDtypeStruct((16, 128, 128), F32),
        ),
        in_specs=[smem, smem, hbm, hbm, vmem, vmem, vmem],
        out_specs=(vmem, vmem),
        scratch_shapes=[
            pltpu.VMEM((8, 576, 256), BF16),
            pltpu.VMEM((576, 2048), BF16),
            pltpu.VMEM((32, 128), jnp.int32),
            pltpu.VMEM((256, 2048), F32),
            pltpu.VMEM((256, 2048), F32),
            pltpu.VMEM((256, 128), F32),
            pltpu.VMEM((8, 2, 256), F32),
            pltpu.VMEM((8, 15, 2, 256), F32),
            pltpu.VMEM((8, 2, 16, 2048), F32),
            pltpu.VMEM((8, 16, 2048), F32),
            pltpu.VMEM((4, 16, 2048), F32),
            pltpu.VMEM((3, 16, 2048), F32),
            pltpu.VMEM((128, 128), F32),
            pltpu.VMEM((1024, 128), F32),
            pltpu.VMEM((4, 8, 2048), F32),
            pltpu.VMEM((16, 2048), F32),
            pltpu.VMEM((16, 128), F32),
            pltpu.VMEM((15, 16, 128), F32),
            pltpu.VMEM((128, 128), F32),
            pltpu.VMEM((8, 136, 128), F32),
            pltpu.VMEM((6, 136, 128), F32),
            pltpu.VMEM((136, 128), F32),
            pltpu.VMEM((136, 128), F32),
            pltpu.VMEM((8, 2, 128, 128), F32),
            pltpu.VMEM((8, 128, 128), F32),
            pltpu.VMEM((4, 128, 128), F32),
            pltpu.VMEM((3, 128, 128), F32),
            dma((8,)), dma,
            dma((8,)), dma((8,)), dma, dma,
            dma((8,)), dma((8,)), dma((4,)), dma((4,)), dma((3,)), dma((3,)),
            dma((8,)), dma((8,)), dma, dma, dma((8,)), dma((8,)),
            dma((8,)), dma((8,)), dma((4,)), dma((4,)), dma((3,)), dma((3,)),
            dma((15,)), dma((16,)),
        ],
        compiler_params=pltpu.CompilerParams(
            collective_id=0, has_side_effects=True, vmem_limit_bytes=60 * 1024 * 1024
        ),
        name="fused_indexer_step",
    )(
        query_pos,
        kl_weight,
        jnp.transpose(main_query, (1, 2, 0)),
        jnp.transpose(latent_keys, (1, 0)),
        index_query.reshape(1024, 128),
        index_keys,
        index_weight,
    )
    query_grad, key_grad, weight_grad = pl.pallas_call(
        finish,
        out_shape=(
            jax.ShapeDtypeStruct((1024, 128), F32),
            jax.ShapeDtypeStruct((2048, 128), F32),
            jax.ShapeDtypeStruct((16, 64), F32),
        ),
        in_specs=[vmem, vmem],
        out_specs=(vmem, vmem, vmem),
        name="finish",
    )(query_blocks, key_blocks)
    return query_grad.reshape(16, 64, 128), key_grad, weight_grad


def solution(mesh):
    placed = (
        P(None, "heads", None),
        P("keys", None),
        P("heads", None, None),
        P("keys", None),
        P("heads", None),
        P(),
        P("heads"),
    )
    return jax.shard_map(
        shards,
        mesh=mesh,
        in_specs=placed,
        out_specs=(P("heads", None, None), P("keys", None), P("heads", None)),
        check_vma=False,
    )
```

```python
import functools

import jax
import jax.numpy as jnp
from jax import lax
from jax.experimental import pallas as pl
from jax.experimental.pallas import tpu as pltpu
from jax.sharding import PartitionSpec as P

H = 128
SCALE = 192.0 ** (-0.5)
SCALE2 = SCALE * 1.4426950408889634
MASKED = -1e30
FLOOR = -1e29
HUGE = 1e30
MESH = pl.DeviceIdType.MESH
LAG = 3
NT = (((1,), (1,)), ((), ()))
F32 = jnp.float32
BF16 = jnp.bfloat16


def lanes(t):
    return slice(t * 128, (t + 1) * 128)


def fused(
    pos_s, kl_s, mqt_hbm, lkt_hbm, iq, ik, iw,
    qg_all, kg_all,
    mqt, lkt_in, posb_ref,
    s_a, s_b, st_ref, stat_mine, stat_all,
    tp_ref, tc_ref, tx_ref, ty_ref,
    wpad_ref, wcol_ref, is_ref, ie_ref, ist_mine, ist_all,
    wgc_ref, qg_part, qg_recv, qg_four, qg_xh,
    kp_ref, kc_ref, kx_ref, ky_ref,
    mq_in, lk_in,
    stat_ss, stat_rs, ist_ss, ist_rs,
    tc_ss, tc_rs, tx_ss, tx_rs, ty_ss, ty_rs,
    qg_ss, qg_rs, xh_ss, xh_rs, qa_ss, qa_rs,
    kc_ss, kc_rs, kx_ss, kx_rs, ky_ss, ky_rs, ka_ss, ka_rs,
    lkt, mq_ref, e_ref, lg_ref, iqt_ref, ikc, d_ref, sl_ref,
):
    for i in range(8):
        pltpu.make_async_copy(mqt_hbm.at[i], mqt.at[i], mq_in.at[i]).start()
    pltpu.make_async_copy(lkt_hbm, lkt_in, lk_in).start()
    h = lax.axis_index("heads")
    k = lax.axis_index("keys")
    core, y, x = h % 2, (h // 2) % 4, h // 8
    z, xh = k // 2, k % 2
    key_first = k * 2048
    partner = x * 8 + y * 2 + (1 - core)
    across = (1 - x) * 8 + y * 2 + core

    def along_y(off):
        return x * 8 + ((y + off) % 4) * 2 + core

    def chip(b):
        return ((x + 1 - b // 4) % 2) * 4 + (y + 3 - b % 4) % 4

    barrier = pltpu.get_barrier_semaphore()
    for r in range(1, 16):
        pl.semaphore_signal(barrier, inc=1, device_id={"keys": (k + r) % 16}, device_id_type=MESH)
    for peer in (partner, across, along_y(1), along_y(2), along_y(3)):
        pl.semaphore_signal(barrier, inc=1, device_id={"heads": peer}, device_id_type=MESH)

    lane = lax.broadcasted_iota(jnp.int32, (1, 128), 1)
    sub = lax.broadcasted_iota(jnp.int32, (8, 128), 0)

    ikc[...] = ik[...]

    wpad_ref[...] = jnp.zeros((128, 128), F32)
    wpad_ref[0:16, 0:64] = iw[...]
    wturned = jnp.transpose(wpad_ref[...])
    for q in range(16):
        wcol_ref[q * 64:(q + 1) * 64, :] = jnp.broadcast_to(wturned[0:64, q:q + 1], (64, 128))
    for i in range(8):
        iqt_ref[:, lanes(i)] = jnp.transpose(iq[lanes(i), :].astype(F32) * wcol_ref[lanes(i), :]).astype(BF16)

    def index_step(g, carry):
        rows = pl.ds(pl.multiple_of(g * 256, 256), 256)

        def part(i, inner):
            got = lax.dot_general(
                iq[rows, :], ikc[pl.ds(pl.multiple_of(i * 256, 256), 256), :], NT, preferred_element_type=F32
            )
            for j in range(4):
                qrows = pl.ds(pl.multiple_of(g * 256 + j * 64, 64), 64)
                for t in range(2):
                    cols = pl.ds(pl.multiple_of(i * 256 + t * 128, 128), 128)
                    v = got[j * 64:(j + 1) * 64, lanes(t)]
                    lg_ref[qrows, cols] = v.astype(BF16)
                    is_ref[g, j:j + 1, cols] = jnp.sum(
                        jnp.maximum(v, 0.0) * wcol_ref[qrows, :], axis=0, keepdims=True
                    )
            return inner

        lax.fori_loop(0, 8, part, 0)
        return carry

    lax.fori_loop(0, 2, index_step, 0)

    unit = lax.broadcasted_iota(jnp.int32, (256, 256), 0) == lax.broadcasted_iota(jnp.int32, (256, 256), 1)
    unit = jnp.where(unit, 1.0, 0.0).astype(BF16)

    def turn(i, carry):
        pltpu.make_async_copy(mqt_hbm.at[i], mqt.at[i], mq_in.at[i]).wait()
        got = lax.dot_general(unit, mqt[i], NT, preferred_element_type=F32).astype(BF16)
        for c in range(8):
            mq_ref[c, i] = got[c * 32:(c + 1) * 32, :]
        return carry

    lax.fori_loop(0, 8, turn, 0)
    pltpu.make_async_copy(lkt_hbm, lkt_in, lk_in).wait()

    def settle(i, carry):
        rows = pl.ds(pl.multiple_of(i * 64, 64), 64)
        lkt[rows, :] = lkt_in[rows, :]
        return carry

    lax.fori_loop(0, 9, settle, 0)

    def to_heads(src, dst, ss, rs, peer):
        return pltpu.make_async_remote_copy(
            src_ref=src, dst_ref=dst, send_sem=ss, recv_sem=rs,
            device_id={"heads": peer}, device_id_type=MESH,
        )

    def to_keys(src, dst, ss, rs, peer):
        return pltpu.make_async_remote_copy(
            src_ref=src, dst_ref=dst, send_sem=ss, recv_sem=rs,
            device_id={"keys": peer}, device_id_type=MESH,
        )

    def take(ref, sem):
        pltpu.make_async_copy(ref, ref, sem).wait()

    def score_quarter(b, i, s_ref):
        cols = pl.ds(pl.multiple_of(i * 512, 512), 512)
        s_ref[:, cols] = jnp.dot(
            mq_ref[chip(b)].reshape(256, 576), lkt[:, cols], preferred_element_type=F32
        )

    def soft_piece(b, i, s_ref):
        r0 = pl.multiple_of(chip(b) * 256, 256)
        rows = pl.ds(pl.multiple_of(i * 64, 64), 64)
        reach = jnp.concatenate([posb_ref[...]] * 2, axis=0)
        top = jnp.full((64, 128), FLOOR, F32)
        for t in range(16):
            v = jnp.minimum(s_ref[rows, lanes(t)], reach + (0.5 - t * 128) * HUGE)
            s_ref[rows, lanes(t)] = v
            top = jnp.maximum(top, v)
        mcol = jnp.broadcast_to(jnp.max(top, axis=1, keepdims=True), (64, 128))
        total = jnp.zeros((64, 128), F32)
        erows = pl.ds(pl.multiple_of(r0 + i * 64, 64), 64)
        for t in range(16):
            e = jnp.exp2((s_ref[rows, lanes(t)] - mcol) * SCALE2)
            total = total + e
            e_ref[erows, lanes(t)] = e.astype(BF16)
        lcol = jnp.broadcast_to(jnp.sum(total, axis=1, keepdims=True), (64, 128))
        st_ref[rows, :] = jnp.where(lane == 0, mcol, lcol)

    def reach_of(b):
        for n in range(4):
            got = jnp.zeros((8, 128), jnp.int32)
            for j in range(8):
                got = jnp.where(sub == j, pos_s[chip(b) * 32 + n * 8 + j] - key_first, got)
            posb_ref[n * 8:(n + 1) * 8, :] = (got - lane).astype(F32) * HUGE

    def send_stats(b):
        stat_mine[b] = jnp.transpose(st_ref[...])[0:2, :]
        for r in range(1, 16):
            to_keys(stat_mine.at[b], stat_all.at[b, r - 1], stat_ss.at[b], stat_rs.at[b], (k + r) % 16).start()

    def target_block(b):
        take(stat_all.at[b], stat_rs.at[b])
        mine = stat_mine[b]
        m0, l0 = mine[0:1, :], mine[1:2, :]
        ms = [stat_all[b, r][0:1, :] for r in range(15)]
        ls = [stat_all[b, r][1:2, :] for r in range(15)]
        top = m0
        for m in ms:
            top = jnp.maximum(top, m)
        share = jnp.exp((m0 - top) * SCALE)
        total = l0 * share
        for m, l in zip(ms, ls):
            total = total + l * jnp.exp((m - top) * SCALE)
        w = share / (total * float(H))
        high = w.astype(BF16).astype(F32)
        low = w - high
        mine_of = lax.broadcasted_iota(jnp.int32, (32, 256), 1) % 32 == lax.broadcasted_iota(
            jnp.int32, (32, 256), 0
        )
        a = jnp.concatenate([jnp.where(mine_of, high, 0.0), jnp.where(mine_of, low, 0.0)], axis=0)
        r0 = pl.multiple_of(chip(b) * 256, 256)
        got = jnp.dot(a.astype(BF16), e_ref[pl.ds(r0, 256), :], preferred_element_type=F32)
        got = got[0:32, :] + got[32:64, :]
        tp_ref[b, 0] = got[0:16, :]
        tp_ref[b, 1] = got[16:32, :]
        to_heads(tp_ref.at[b, 1 - core], tc_ref.at[b], tc_ss.at[b], tc_rs.at[b], partner).start()

    def cross_x(b, p_ref, c_ref, x_ref, c_rs, x_ss, x_rs):
        take(c_ref.at[b], c_rs.at[b])
        p_ref[b, core] = p_ref[b, core] + c_ref[b]
        to_heads(p_ref.at[b, core], x_ref.at[b], x_ss.at[b], x_rs.at[b], across).start()

    def cross_y(i, p_ref, c_ref, x_ref, y_ref, c_rs, x_rs, y_ss, y_rs):
        b = 4 + i
        take(c_ref.at[b], c_rs.at[b])
        take(x_ref.at[i], x_rs.at[i])
        p_ref[b, core] = p_ref[b, core] + c_ref[b] + x_ref[i]
        off = 3 - i
        if off:
            to_heads(
                p_ref.at[b, core], y_ref.at[off - 1], y_ss.at[off - 1], y_rs.at[off - 1], along_y(off)
            ).start()

    def first(i, carry):
        score_quarter(0, i, s_a)
        return carry

    lax.fori_loop(0, 4, first, 0)
    pl.semaphore_wait(barrier, 20)

    def one_block(b, s_now, s_next):
        reach_of(b)

        for i in range(4):
            soft_piece(b, i, s_now)
            score_quarter(jnp.minimum(b + 1, 7), i, s_next)
        send_stats(b)

        @pl.when(b >= LAG)
        def _():
            target_block(b - LAG)

        @pl.when(b >= LAG + 1)
        def _():
            cross_x(b - LAG - 1, tp_ref, tc_ref, tx_ref, tc_rs, tx_ss, tx_rs)

    def two_blocks(n, carry):
        one_block(n * 2, s_a, s_b)
        one_block(n * 2 + 1, s_b, s_a)
        return carry

    lax.fori_loop(0, 4, two_blocks, 0)

    def own_chip(i):
        cross_y(i, tp_ref, tc_ref, tx_ref, ty_ref, tc_rs, tx_rs, ty_ss, ty_rs)

    target_block(5)

    def index_rest(g, carry):
        index_step(g, carry)

        @pl.when(g == 2)
        def _():
            own_chip(0)

        return carry

    lax.fori_loop(2, 4, index_rest, 0)
    own_chip(1)

    row = lax.broadcasted_iota(jnp.int32, (16, 128), 0)
    posr = jnp.zeros((16, 128), jnp.int32)
    klr = jnp.zeros((16, 128), F32)
    for q in range(16):
        posr = jnp.where(row == q, pos_s[h * 16 + q] - key_first, posr)
        klr = jnp.where(row == q, kl_s[q], klr)
    top = jnp.full((16, 128), FLOOR, F32)
    for t in range(16):
        v = jnp.concatenate([is_ref[g, 0:4, lanes(t)] for g in range(4)], axis=0)
        v = jnp.where(lane + t * 128 <= posr, v, MASKED)
        ie_ref[:, lanes(t)] = v
        top = jnp.maximum(top, v)
    im = jnp.broadcast_to(jnp.max(top, axis=1, keepdims=True), (16, 128))
    total = jnp.zeros((16, 128), F32)
    for t in range(16):
        e = jnp.exp(ie_ref[:, lanes(t)] - im)
        total = total + e
        ie_ref[:, lanes(t)] = e
    il = jnp.broadcast_to(jnp.sum(total, axis=1, keepdims=True), (16, 128))
    ist_mine[...] = jnp.where(lane == 0, im, il)
    for r in range(1, 16):
        to_keys(ist_mine, ist_all.at[r - 1], ist_ss, ist_rs, (k + r) % 16).start()

    target_block(6)
    target_block(7)
    own_chip(2)
    own_chip(3)

    take(ist_all, ist_rs)
    ms = [jnp.broadcast_to(ist_all[r][:, 0:1], (16, 128)) for r in range(15)]
    top = im
    for m in ms:
        top = jnp.maximum(top, m)
    share = jnp.exp(im - top)
    total = il * share
    for r in range(15):
        total = total + jnp.broadcast_to(ist_all[r][:, 1:2], (16, 128)) * jnp.exp(ms[r] - top)
    share = share / total

    for j in range(3):
        take(ty_ref.at[j], ty_rs.at[j])
    for t in range(16):
        target = tp_ref[7, core, :, lanes(t)]
        for j in range(3):
            target = target + ty_ref[j, :, lanes(t)]
        delta = klr * (ie_ref[:, lanes(t)] * share - target)
        for q in range(16):
            d_ref[q, :, lanes(t)] = jnp.broadcast_to(delta[q:q + 1, :], (16, 128)).astype(BF16)

    def z_peer(off):
        return ((z + off) % 8) * 2 + xh

    def back_step(offsets):
        picked = []
        for off in offsets:
            q0 = ((z + off) % 8) * 2
            for j in range(2):
                qrows = pl.ds(pl.multiple_of((q0 + j) * 64, 64), 64)
                for t in range(16):
                    d = jnp.concatenate([d_ref[q0 + j, :, lanes(t)]] * 4, axis=0)
                    sl_ref[qrows, lanes(t)] = jnp.where(
                        lg_ref[qrows, lanes(t)] > 0, d, jnp.zeros((64, 128), BF16)
                    )
            picked.append(pl.ds(pl.multiple_of(q0 * 64, 128), 128))
        gate = jnp.concatenate([sl_ref[rows, :] for rows in picked], axis=0)
        both = jnp.dot(gate, ikc[...], preferred_element_type=F32)
        columns = jnp.zeros((64, 128), F32)
        for n, (off, rows) in enumerate(zip(offsets, picked)):
            got = both[n * 128:(n + 1) * 128, :]
            along = jnp.sum(got * iq[rows, :].astype(F32), axis=1, keepdims=True)
            for j in range(2):
                columns = jnp.where(
                    lane == n * 8 + j, jnp.broadcast_to(along[j * 64:(j + 1) * 64], (64, 128)), columns
                )
            qg_part[off, 0:128, :] = got * wcol_ref[rows, :]
        wgc_ref[0:64, :] = columns
        turned = jnp.transpose(wgc_ref[...])
        for n, off in enumerate(offsets):
            qg_part[off, 128:136, :] = turned[n * 8:(n + 1) * 8, :]

    def z_send(src, dst, n, off):
        to_keys(src, dst, qg_ss.at[n], qg_rs.at[n], z_peer(off)).start()

    wgc_ref[...] = jnp.zeros((128, 128), F32)
    back_step((4, 3))
    z_send(qg_part.at[4, 0:72], qg_four.at[0:72], 0, 2)
    z_send(qg_part.at[4, 72:136], qg_four.at[72:136], 1, 6)
    z_send(qg_part.at[3], qg_recv.at[0], 2, 1)
    back_step((5, 2))
    z_send(qg_part.at[5], qg_recv.at[1], 3, 7)
    back_step((6, 1))
    z_send(qg_part.at[1], qg_recv.at[2], 4, 1)
    back_step((7, 0))
    z_send(qg_part.at[7], qg_recv.at[3], 5, 7)

    def z_join():
        take(qg_recv.at[0], qg_rs.at[2])
        take(qg_four.at[0:72], qg_rs.at[0])
        qg_part[2, 0:72, :] = qg_part[2, 0:72, :] + qg_recv[0, 0:72, :] + qg_four[0:72, :]
        qg_part[2, 72:136, :] = qg_part[2, 72:136, :] + qg_recv[0, 72:136, :]
        z_send(qg_part.at[2], qg_recv.at[4], 6, 2)
        take(qg_recv.at[1], qg_rs.at[3])
        take(qg_four.at[72:136], qg_rs.at[1])
        qg_part[6, 0:72, :] = qg_part[6, 0:72, :] + qg_recv[1, 0:72, :]
        qg_part[6, 72:136, :] = qg_part[6, 72:136, :] + qg_recv[1, 72:136, :] + qg_four[72:136, :]
        z_send(qg_part.at[6], qg_recv.at[5], 7, 6)

    def key_step(b, carry):
        cols = pl.ds(pl.multiple_of(chip(b) * 256, 256), 256)
        got = jnp.dot(iqt_ref[...], sl_ref[:, cols], preferred_element_type=F32)
        kp_ref[b, 0] = got[:, 0:128]
        kp_ref[b, 1] = got[:, 128:256]
        to_heads(kp_ref.at[b, 1 - core], kc_ref.at[b], kc_ss.at[b], kc_rs.at[b], partner).start()

        @pl.when(b >= 4)
        def _():
            cross_x(b - 4, kp_ref, kc_ref, kx_ref, kc_rs, kx_ss, kx_rs)

        return carry

    lax.fori_loop(0, 8, key_step, 0)
    z_join()

    for i in range(4):
        cross_y(i, kp_ref, kc_ref, kx_ref, ky_ref, kc_rs, kx_rs, ky_ss, ky_rs)

    for j in range(4):
        take(qg_recv.at[2 + j], qg_rs.at[4 + j])
    qg_part[0] = qg_part[0] + (qg_recv[2] + qg_recv[3]) + (qg_recv[4] + qg_recv[5])
    to_keys(qg_part.at[0], qg_xh, xh_ss, xh_rs, z * 2 + (1 - xh)).start()

    for j in range(3):
        take(ky_ref.at[j], ky_rs.at[j])
    shard = kp_ref[7, core]
    for j in range(3):
        shard = shard + ky_ref[j]
    kg_all[h] = jnp.transpose(shard)

    def pass_on(s, peer, n):
        to_heads(kg_all.at[s], kg_all.at[s], ka_ss.at[n], ka_rs.at[s], peer).start()

    for off in (1, 2, 3):
        pass_on(h, along_y(off), off - 1)
    pass_on(h, across, 3)
    pass_on(h, partner, 4)

    def z_back(off_from, part, n, off):
        ref = qg_all.at[(z + off_from) % 8, part]
        to_keys(ref, ref, qa_ss.at[n], qa_rs.at[n], z_peer(off)).start()

    def z_take(off_from, part, n):
        take(qg_all.at[(z + off_from) % 8, part], qa_rs.at[n])

    whole, front, rear = slice(0, 136), slice(0, 72), slice(72, 136)
    take(qg_xh, xh_rs)
    qg_all[z] = qg_part[0] + qg_xh[...]
    z_back(0, whole, 0, 2)
    z_back(0, whole, 1, 6)
    z_back(0, whole, 2, 1)
    z_back(0, whole, 3, 7)
    for off in (1, 3, 2):
        s = along_y(off)
        take(kg_all.at[s], ka_rs.at[s])
        pass_on(s, across, 4 + off)
        pass_on(s, partner, 7 + off)
    z_take(6, whole, 0)
    z_back(6, front, 4, 2)
    z_back(6, whole, 5, 1)
    z_take(2, whole, 1)
    z_back(2, rear, 6, 6)
    z_back(2, whole, 7, 7)
    for off in (0, 1, 3, 2):
        s = (1 - x) * 8 + ((y + off) % 4) * 2 + core
        take(kg_all.at[s], ka_rs.at[s])
        pass_on(s, partner, 11 + off)

    z_take(7, whole, 2)
    z_take(1, whole, 3)
    z_take(4, front, 4)
    z_take(5, whole, 5)
    z_take(4, rear, 6)
    z_take(3, whole, 7)
    for c in range(8):
        s = c * 2 + (1 - core)
        take(kg_all.at[s], ka_rs.at[s])

    for b in range(8):
        take(stat_all.at[b], stat_ss.at[b])
        take(tc_ref.at[b], tc_ss.at[b])
        take(kc_ref.at[b], kc_ss.at[b])
    take(ist_all, ist_ss)
    for b in range(4):
        take(tx_ref.at[b], tx_ss.at[b])
        take(kx_ref.at[b], kx_ss.at[b])
    for j in range(3):
        take(ty_ref.at[j], ty_ss.at[j])
        take(ky_ref.at[j], ky_ss.at[j])
    take(qg_four.at[0:72], qg_ss.at[0])
    take(qg_four.at[72:136], qg_ss.at[1])
    for j in range(6):
        take(qg_recv.at[j], qg_ss.at[2 + j])
    for n, part in enumerate((whole, whole, whole, whole, front, whole, rear, whole)):
        take(qg_all.at[0, part], qa_ss.at[n])
    take(qg_xh, xh_ss)
    for n in range(15):
        take(kg_all.at[n], ka_ss.at[n])


def scoped(*refs):
    pl.run_scoped(
        functools.partial(fused, *refs),
        pltpu.VMEM((576, 2048), BF16),
        pltpu.VMEM((8, 8, 32, 576), BF16),
        pltpu.VMEM((2048, 2048), BF16),
        pltpu.VMEM((1024, 2048), BF16),
        pltpu.VMEM((128, 1024), BF16),
        pltpu.VMEM((2048, 128), BF16),
        pltpu.VMEM((16, 16, 2048), BF16),
        pltpu.VMEM((1024, 2048), BF16),
    )


def finish(qg_all, kg_all, qg_out, kg_out, wg_out):
    for i in range(2):
        qg_out[i * 128:(i + 1) * 128, :] = qg_all[i, 0:128, :]
    for i in range(4):
        kg_out[i * 128:(i + 1) * 128, :] = kg_all[i]
    for n in range(4):

        @pl.when(pl.program_id(0) == n)
        def _():
            for i in range(2):
                wg_out[n * 4 + i * 2:n * 4 + (i + 1) * 2, :] = qg_all[i, 128:130, 0:64]


def shards(main_query, latent_keys, index_query, index_keys, index_weight, query_pos, kl_weight):
    vmem = pl.BlockSpec(memory_space=pltpu.VMEM)
    smem = pl.BlockSpec(memory_space=pltpu.SMEM)
    hbm = pl.BlockSpec(memory_space=pl.ANY)
    dma = pltpu.SemaphoreType.DMA
    query_blocks, key_blocks = pl.pallas_call(
        scoped,
        out_shape=(
            jax.ShapeDtypeStruct((8, 136, 128), F32),
            jax.ShapeDtypeStruct((16, 128, 128), F32),
        ),
        in_specs=[smem, smem, hbm, hbm, vmem, vmem, vmem],
        out_specs=(vmem, vmem),
        scratch_shapes=[
            pltpu.VMEM((8, 576, 256), BF16),
            pltpu.VMEM((576, 2048), BF16),
            pltpu.VMEM((32, 128), F32),
            pltpu.VMEM((256, 2048), F32),
            pltpu.VMEM((256, 2048), F32),
            pltpu.VMEM((256, 128), F32),
            pltpu.VMEM((8, 2, 256), F32),
            pltpu.VMEM((8, 15, 2, 256), F32),
            pltpu.VMEM((8, 2, 16, 2048), F32),
            pltpu.VMEM((8, 16, 2048), F32),
            pltpu.VMEM((4, 16, 2048), F32),
            pltpu.VMEM((3, 16, 2048), F32),
            pltpu.VMEM((128, 128), F32),
            pltpu.VMEM((1024, 128), F32),
            pltpu.VMEM((4, 8, 2048), F32),
            pltpu.VMEM((16, 2048), F32),
            pltpu.VMEM((16, 128), F32),
            pltpu.VMEM((15, 16, 128), F32),
            pltpu.VMEM((128, 128), F32),
            pltpu.VMEM((8, 136, 128), F32),
            pltpu.VMEM((6, 136, 128), F32),
            pltpu.VMEM((136, 128), F32),
            pltpu.VMEM((136, 128), F32),
            pltpu.VMEM((8, 2, 128, 128), F32),
            pltpu.VMEM((8, 128, 128), F32),
            pltpu.VMEM((4, 128, 128), F32),
            pltpu.VMEM((3, 128, 128), F32),
            dma((8,)), dma,
            dma((8,)), dma((8,)), dma, dma,
            dma((8,)), dma((8,)), dma((4,)), dma((4,)), dma((3,)), dma((3,)),
            dma((8,)), dma((8,)), dma, dma, dma((8,)), dma((8,)),
            dma((8,)), dma((8,)), dma((4,)), dma((4,)), dma((3,)), dma((3,)),
            dma((15,)), dma((16,)),
        ],
        compiler_params=pltpu.CompilerParams(
            collective_id=0, has_side_effects=True, vmem_limit_bytes=60 * 1024 * 1024
        ),
        name="fused_indexer_step",
    )(
        query_pos,
        kl_weight,
        jnp.transpose(main_query, (1, 2, 0)),
        jnp.transpose(latent_keys, (1, 0)),
        index_query.reshape(1024, 128),
        index_keys,
        index_weight,
    )
    query_grad, key_grad, weight_grad = pl.pallas_call(
        finish,
        out_shape=(
            jax.ShapeDtypeStruct((1024, 128), F32),
            jax.ShapeDtypeStruct((2048, 128), F32),
            jax.ShapeDtypeStruct((16, 64), F32),
        ),
        grid=(4,),
        in_specs=[
            pl.BlockSpec((2, 136, 128), lambda n: (n, 0, 0)),
            pl.BlockSpec((4, 128, 128), lambda n: (n, 0, 0)),
        ],
        out_specs=(
            pl.BlockSpec((256, 128), lambda n: (n, 0)),
            pl.BlockSpec((512, 128), lambda n: (n, 0)),
            pl.BlockSpec((16, 64), lambda n: (0, 0)),
        ),
        name="finish",
    )(query_blocks, key_blocks)
    return query_grad.reshape(16, 64, 128), key_grad, weight_grad


def solution(mesh):
    placed = (
        P(None, "heads", None),
        P("keys", None),
        P("heads", None, None),
        P("keys", None),
        P("heads", None),
        P(),
        P("heads"),
    )
    return jax.shard_map(
        shards,
        mesh=mesh,
        in_specs=placed,
        out_specs=(P("heads", None, None), P("keys", None), P("heads", None)),
        check_vma=False,
    )
```

```python
import functools

import jax
import jax.numpy as jnp
from jax import lax
from jax.experimental import pallas as pl
from jax.experimental.pallas import tpu as pltpu
from jax.sharding import PartitionSpec as P

H = 128
SCALE = 192.0 ** (-0.5)
SCALE2 = SCALE * 1.4426950408889634
MASKED = -1e30
FLOOR = -1e29
HUGE = 1e30
MESH = pl.DeviceIdType.MESH
LAG = 3
NT = (((1,), (1,)), ((), ()))
F32 = jnp.float32
BF16 = jnp.bfloat16


def lanes(t):
    return slice(t * 128, (t + 1) * 128)


def fused(
    pos_s, kl_s, mqt_hbm, lkt_hbm, iq, ik, iw,
    qg_all, kg_all,
    mqt, lkt_in, posb_ref,
    s_a, s_b, st_ref, stat_mine, stat_all,
    tp_ref, tc_ref, tx_ref, ty_ref,
    wpad_ref, wcol_ref, is_ref, ie_ref, ist_mine, ist_all,
    wgc_ref, qg_part, qg_recv, qg_four, qg_xh,
    kp_ref, kc_ref, kx_ref, ky_ref,
    mq_in, lk_in,
    stat_ss, stat_rs, ist_ss, ist_rs,
    tc_ss, tc_rs, tx_ss, tx_rs, ty_ss, ty_rs,
    qg_ss, qg_rs, xh_ss, xh_rs, qa_ss, qa_rs,
    kc_ss, kc_rs, kx_ss, kx_rs, ky_ss, ky_rs, ka_ss, ka_rs,
    lkt, mq_ref, e_ref, lg_ref, iqt_ref, ikc, d_ref, sl_ref, ikt,
):
    for i in range(8):
        pltpu.make_async_copy(mqt_hbm.at[i], mqt.at[i], mq_in.at[i]).start()
    pltpu.make_async_copy(lkt_hbm, lkt_in, lk_in).start()
    h = lax.axis_index("heads")
    k = lax.axis_index("keys")
    core, y, x = h % 2, (h // 2) % 4, h // 8
    z, xh = k // 2, k % 2
    key_first = k * 2048
    partner = x * 8 + y * 2 + (1 - core)
    across = (1 - x) * 8 + y * 2 + core

    def along_y(off):
        return x * 8 + ((y + off) % 4) * 2 + core

    def chip(b):
        return ((x + 1 - b // 4) % 2) * 4 + (y + 3 - b % 4) % 4

    barrier = pltpu.get_barrier_semaphore()
    for r in range(1, 16):
        pl.semaphore_signal(barrier, inc=1, device_id={"keys": (k + r) % 16}, device_id_type=MESH)
    for peer in (partner, across, along_y(1), along_y(2), along_y(3)):
        pl.semaphore_signal(barrier, inc=1, device_id={"heads": peer}, device_id_type=MESH)

    lane = lax.broadcasted_iota(jnp.int32, (1, 128), 1)
    sub = lax.broadcasted_iota(jnp.int32, (8, 128), 0)

    ikc[...] = ik[...]

    wpad_ref[...] = jnp.zeros((128, 128), F32)
    wpad_ref[0:16, 0:64] = iw[...]
    wturned = jnp.transpose(wpad_ref[...])
    for q in range(16):
        wcol_ref[q * 64:(q + 1) * 64, :] = jnp.broadcast_to(wturned[0:64, q:q + 1], (64, 128))
    def index_part(g, i):
        rows = pl.ds(pl.multiple_of(g * 256, 256), 256)
        got = lax.dot_general(
            iq[rows, :], ikc[pl.ds(pl.multiple_of(i * 256, 256), 256), :], NT, preferred_element_type=F32
        )
        for j in range(4):
            qrows = pl.ds(pl.multiple_of(g * 256 + j * 64, 64), 64)
            for t in range(2):
                cols = pl.ds(pl.multiple_of(i * 256 + t * 128, 128), 128)
                v = got[j * 64:(j + 1) * 64, lanes(t)]
                lg_ref[qrows, cols] = v.astype(BF16)
                is_ref[g, j:j + 1, cols] = jnp.sum(
                    jnp.maximum(v, 0.0) * wcol_ref[qrows, :], axis=0, keepdims=True
                )

    unit = lax.broadcasted_iota(jnp.int32, (256, 256), 0) == lax.broadcasted_iota(jnp.int32, (256, 256), 1)
    unit = jnp.where(unit, 1.0, 0.0).astype(BF16)

    def turn(i, carry):
        pltpu.make_async_copy(mqt_hbm.at[i], mqt.at[i], mq_in.at[i]).wait()
        got = lax.dot_general(unit, mqt[i], NT, preferred_element_type=F32).astype(BF16)
        for c in range(8):
            mq_ref[c, i] = got[c * 32:(c + 1) * 32, :]
        index_part(0, i)
        index_part(1, i)
        return carry

    lax.fori_loop(0, 8, turn, 0)
    pltpu.make_async_copy(lkt_hbm, lkt_in, lk_in).wait()

    def settle(i, carry):
        rows = pl.ds(pl.multiple_of(i * 64, 64), 64)
        lkt[rows, :] = lkt_in[rows, :]
        return carry

    lax.fori_loop(0, 9, settle, 0)

    def to_heads(src, dst, ss, rs, peer):
        return pltpu.make_async_remote_copy(
            src_ref=src, dst_ref=dst, send_sem=ss, recv_sem=rs,
            device_id={"heads": peer}, device_id_type=MESH,
        )

    def to_keys(src, dst, ss, rs, peer):
        return pltpu.make_async_remote_copy(
            src_ref=src, dst_ref=dst, send_sem=ss, recv_sem=rs,
            device_id={"keys": peer}, device_id_type=MESH,
        )

    def take(ref, sem):
        pltpu.make_async_copy(ref, ref, sem).wait()

    def score_quarter(b, i, s_ref):
        cols = pl.ds(pl.multiple_of(i * 512, 512), 512)
        s_ref[:, cols] = jnp.dot(
            mq_ref[chip(b)].reshape(256, 576), lkt[:, cols], preferred_element_type=F32
        )

    def soft_piece(b, i, s_ref):
        r0 = pl.multiple_of(chip(b) * 256, 256)
        rows = pl.ds(pl.multiple_of(i * 32, 32), 32)
        reach = posb_ref[...]
        top = jnp.full((32, 128), FLOOR, F32)
        for t in range(16):
            v = jnp.minimum(s_ref[rows, lanes(t)], reach + (0.5 - t * 128) * HUGE)
            s_ref[rows, lanes(t)] = v
            top = jnp.maximum(top, v)
        mcol = jnp.broadcast_to(jnp.max(top, axis=1, keepdims=True), (32, 128))
        total = jnp.zeros((32, 128), F32)
        erows = pl.ds(pl.multiple_of(r0 + i * 32, 32), 32)
        for t in range(16):
            e = jnp.exp2((s_ref[rows, lanes(t)] - mcol) * SCALE2)
            total = total + e
            e_ref[erows, lanes(t)] = e.astype(BF16)
        lcol = jnp.broadcast_to(jnp.sum(total, axis=1, keepdims=True), (32, 128))
        st_ref[rows, :] = jnp.where(lane == 0, mcol, lcol)

    def reach_of(b):
        for n in range(4):
            got = jnp.zeros((8, 128), jnp.int32)
            for j in range(8):
                got = jnp.where(sub == j, pos_s[chip(b) * 32 + n * 8 + j] - key_first, got)
            posb_ref[n * 8:(n + 1) * 8, :] = (got - lane).astype(F32) * HUGE

    def send_stats(b):
        stat_mine[b] = jnp.transpose(st_ref[...])[0:2, :]
        for r in range(1, 16):
            to_keys(stat_mine.at[b], stat_all.at[b, r - 1], stat_ss.at[b], stat_rs.at[b], (k + r) % 16).start()

    def target_block(b):
        take(stat_all.at[b], stat_rs.at[b])
        mine = stat_mine[b]
        m0, l0 = mine[0:1, :], mine[1:2, :]
        ms = [stat_all[b, r][0:1, :] for r in range(15)]
        ls = [stat_all[b, r][1:2, :] for r in range(15)]
        top = m0
        for m in ms:
            top = jnp.maximum(top, m)
        share = jnp.exp((m0 - top) * SCALE)
        total = l0 * share
        for m, l in zip(ms, ls):
            total = total + l * jnp.exp((m - top) * SCALE)
        w = share / (total * float(H))
        high = w.astype(BF16).astype(F32)
        low = w - high
        mine_of = lax.broadcasted_iota(jnp.int32, (32, 256), 1) % 32 == lax.broadcasted_iota(
            jnp.int32, (32, 256), 0
        )
        a = jnp.concatenate([jnp.where(mine_of, high, 0.0), jnp.where(mine_of, low, 0.0)], axis=0)
        r0 = pl.multiple_of(chip(b) * 256, 256)
        got = jnp.dot(a.astype(BF16), e_ref[pl.ds(r0, 256), :], preferred_element_type=F32)
        got = got[0:32, :] + got[32:64, :]
        tp_ref[b, 0] = got[0:16, :]
        tp_ref[b, 1] = got[16:32, :]
        to_heads(tp_ref.at[b, 1 - core], tc_ref.at[b], tc_ss.at[b], tc_rs.at[b], partner).start()

    def cross_x(b, p_ref, c_ref, x_ref, c_rs, x_ss, x_rs):
        take(c_ref.at[b], c_rs.at[b])
        p_ref[b, core] = p_ref[b, core] + c_ref[b]
        to_heads(p_ref.at[b, core], x_ref.at[b], x_ss.at[b], x_rs.at[b], across).start()

    def cross_y(i, p_ref, c_ref, x_ref, y_ref, c_rs, x_rs, y_ss, y_rs):
        b = 4 + i
        take(c_ref.at[b], c_rs.at[b])
        take(x_ref.at[i], x_rs.at[i])
        p_ref[b, core] = p_ref[b, core] + c_ref[b] + x_ref[i]
        off = 3 - i
        if off:
            to_heads(
                p_ref.at[b, core], y_ref.at[off - 1], y_ss.at[off - 1], y_rs.at[off - 1], along_y(off)
            ).start()

    def first(i, carry):
        score_quarter(0, i, s_a)
        for j in range(2):
            rows = pl.ds(pl.multiple_of(i * 256 + j * 128, 128), 128)
            iqt_ref[:, rows] = jnp.transpose(iq[rows, :].astype(F32) * wcol_ref[rows, :]).astype(BF16)
        return carry

    lax.fori_loop(0, 4, first, 0)
    pl.semaphore_wait(barrier, 20)

    def one_block(b, s_now, s_next):
        reach_of(b)

        for i in range(4):
            soft_piece(b, i * 2, s_now)
            score_quarter(jnp.minimum(b + 1, 7), i, s_next)
            soft_piece(b, i * 2 + 1, s_now)
        send_stats(b)

        @pl.when(b >= LAG)
        def _():
            target_block(b - LAG)

        @pl.when(b >= LAG + 1)
        def _():
            cross_x(b - LAG - 1, tp_ref, tc_ref, tx_ref, tc_rs, tx_ss, tx_rs)

    def two_blocks(n, carry):
        one_block(n * 2, s_a, s_b)
        one_block(n * 2 + 1, s_b, s_a)
        return carry

    lax.fori_loop(0, 4, two_blocks, 0)

    def own_chip(i):
        cross_y(i, tp_ref, tc_ref, tx_ref, ty_ref, tc_rs, tx_rs, ty_ss, ty_rs)

    target_block(5)

    def index_rest(i, carry):
        index_part(2, i)
        index_part(3, i)

        @pl.when(i == 4)
        def _():
            own_chip(0)

        return carry

    lax.fori_loop(0, 8, index_rest, 0)
    own_chip(1)

    row = lax.broadcasted_iota(jnp.int32, (16, 128), 0)
    posr = jnp.zeros((16, 128), jnp.int32)
    klr = jnp.zeros((16, 128), F32)
    for q in range(16):
        posr = jnp.where(row == q, pos_s[h * 16 + q] - key_first, posr)
        klr = jnp.where(row == q, kl_s[q], klr)
    top = jnp.full((16, 128), FLOOR, F32)
    for t in range(16):
        v = jnp.concatenate([is_ref[g, 0:4, lanes(t)] for g in range(4)], axis=0)
        v = jnp.where(lane + t * 128 <= posr, v, MASKED)
        ie_ref[:, lanes(t)] = v
        top = jnp.maximum(top, v)
    im = jnp.broadcast_to(jnp.max(top, axis=1, keepdims=True), (16, 128))
    total = jnp.zeros((16, 128), F32)
    for t in range(16):
        e = jnp.exp(ie_ref[:, lanes(t)] - im)
        total = total + e
        ie_ref[:, lanes(t)] = e
    il = jnp.broadcast_to(jnp.sum(total, axis=1, keepdims=True), (16, 128))
    ist_mine[...] = jnp.where(lane == 0, im, il)
    for r in range(1, 16):
        to_keys(ist_mine, ist_all.at[r - 1], ist_ss, ist_rs, (k + r) % 16).start()

    def turn_keys(i, carry):
        for j in range(4):
            rows = pl.ds(pl.multiple_of(i * 512 + j * 128, 128), 128)
            ikt[:, rows] = jnp.transpose(ik[rows, :].astype(F32)).astype(BF16)
        return carry

    lax.fori_loop(0, 4, turn_keys, 0)
    target_block(6)
    target_block(7)
    own_chip(2)
    own_chip(3)

    take(ist_all, ist_rs)
    ms = [jnp.broadcast_to(ist_all[r][:, 0:1], (16, 128)) for r in range(15)]
    top = im
    for m in ms:
        top = jnp.maximum(top, m)
    share = jnp.exp(im - top)
    total = il * share
    for r in range(15):
        total = total + jnp.broadcast_to(ist_all[r][:, 1:2], (16, 128)) * jnp.exp(ms[r] - top)
    share = share / total

    for j in range(3):
        take(ty_ref.at[j], ty_rs.at[j])
    for t in range(16):
        target = tp_ref[7, core, :, lanes(t)]
        for j in range(3):
            target = target + ty_ref[j, :, lanes(t)]
        delta = klr * (ie_ref[:, lanes(t)] * share - target)
        for q in range(16):
            d_ref[q, :, lanes(t)] = jnp.broadcast_to(delta[q:q + 1, :], (16, 128)).astype(BF16)

    def z_peer(off):
        return ((z + off) % 8) * 2 + xh

    def back_step(offsets):
        picked = []
        for off in offsets:
            q0 = ((z + off) % 8) * 2
            for j in range(2):
                qrows = pl.ds(pl.multiple_of((q0 + j) * 64, 64), 64)
                for t in range(16):
                    d = jnp.concatenate([d_ref[q0 + j, :, lanes(t)]] * 4, axis=0)
                    sl_ref[qrows, lanes(t)] = jnp.where(
                        lg_ref[qrows, lanes(t)] > 0, d, jnp.zeros((64, 128), BF16)
                    )
            picked.append(pl.ds(pl.multiple_of(q0 * 64, 128), 128))
        gate = jnp.concatenate([sl_ref[rows, :] for rows in picked], axis=0)
        both = jnp.transpose(lax.dot_general(ikt[...], gate, NT, preferred_element_type=F32))
        columns = jnp.zeros((64, 128), F32)
        for n, (off, rows) in enumerate(zip(offsets, picked)):
            got = both[n * 128:(n + 1) * 128, :]
            along = jnp.sum(got * iq[rows, :].astype(F32), axis=1, keepdims=True)
            for j in range(2):
                columns = jnp.where(
                    lane == n * 8 + j, jnp.broadcast_to(along[j * 64:(j + 1) * 64], (64, 128)), columns
                )
            qg_part[off, 0:128, :] = got * wcol_ref[rows, :]
        wgc_ref[0:64, :] = columns
        turned = jnp.transpose(wgc_ref[...])
        for n, off in enumerate(offsets):
            qg_part[off, 128:136, :] = turned[n * 8:(n + 1) * 8, :]

    def z_send(src, dst, n, off):
        to_keys(src, dst, qg_ss.at[n], qg_rs.at[n], z_peer(off)).start()

    wgc_ref[...] = jnp.zeros((128, 128), F32)
    back_step((4, 3))
    z_send(qg_part.at[4, 0:72], qg_four.at[0:72], 0, 2)
    z_send(qg_part.at[4, 72:136], qg_four.at[72:136], 1, 6)
    z_send(qg_part.at[3], qg_recv.at[0], 2, 1)
    back_step((5, 2))
    z_send(qg_part.at[5], qg_recv.at[1], 3, 7)
    back_step((6, 1))
    z_send(qg_part.at[1], qg_recv.at[2], 4, 1)
    back_step((7, 0))
    z_send(qg_part.at[7], qg_recv.at[3], 5, 7)

    def z_join():
        take(qg_recv.at[0], qg_rs.at[2])
        take(qg_four.at[0:72], qg_rs.at[0])
        qg_part[2, 0:72, :] = qg_part[2, 0:72, :] + qg_recv[0, 0:72, :] + qg_four[0:72, :]
        qg_part[2, 72:136, :] = qg_part[2, 72:136, :] + qg_recv[0, 72:136, :]
        z_send(qg_part.at[2], qg_recv.at[4], 6, 2)
        take(qg_recv.at[1], qg_rs.at[3])
        take(qg_four.at[72:136], qg_rs.at[1])
        qg_part[6, 0:72, :] = qg_part[6, 0:72, :] + qg_recv[1, 0:72, :]
        qg_part[6, 72:136, :] = qg_part[6, 72:136, :] + qg_recv[1, 72:136, :] + qg_four[72:136, :]
        z_send(qg_part.at[6], qg_recv.at[5], 7, 6)

    def key_step(b, carry):
        cols = pl.ds(pl.multiple_of(chip(b) * 256, 256), 256)
        got = jnp.dot(iqt_ref[...], sl_ref[:, cols], preferred_element_type=F32)
        kp_ref[b, 0] = got[:, 0:128]
        kp_ref[b, 1] = got[:, 128:256]
        to_heads(kp_ref.at[b, 1 - core], kc_ref.at[b], kc_ss.at[b], kc_rs.at[b], partner).start()

        @pl.when(b >= 4)
        def _():
            cross_x(b - 4, kp_ref, kc_ref, kx_ref, kc_rs, kx_ss, kx_rs)

        return carry

    lax.fori_loop(0, 8, key_step, 0)
    z_join()

    def key_chip(i):
        cross_y(i, kp_ref, kc_ref, kx_ref, ky_ref, kc_rs, kx_rs, ky_ss, ky_rs)

    for i in range(3):
        key_chip(i)

    for j in range(4):
        take(qg_recv.at[2 + j], qg_rs.at[4 + j])
    qg_part[0] = qg_part[0] + (qg_recv[2] + qg_recv[3]) + (qg_recv[4] + qg_recv[5])
    to_keys(qg_part.at[0], qg_xh, xh_ss, xh_rs, z * 2 + (1 - xh)).start()

    key_chip(3)

    for j in range(3):
        take(ky_ref.at[j], ky_rs.at[j])
    shard = kp_ref[7, core]
    for j in range(3):
        shard = shard + ky_ref[j]
    kg_all[h] = jnp.transpose(shard)

    def pass_on(s, peer, n):
        to_heads(kg_all.at[s], kg_all.at[s], ka_ss.at[n], ka_rs.at[s], peer).start()

    for off in (1, 2, 3):
        pass_on(h, along_y(off), off - 1)
    pass_on(h, across, 3)
    pass_on(h, partner, 4)

    def z_back(off_from, part, n, off):
        ref = qg_all.at[(z + off_from) % 8, part]
        to_keys(ref, ref, qa_ss.at[n], qa_rs.at[n], z_peer(off)).start()

    def z_take(off_from, part, n):
        take(qg_all.at[(z + off_from) % 8, part], qa_rs.at[n])

    whole, front, rear = slice(0, 136), slice(0, 72), slice(72, 136)
    take(qg_xh, xh_rs)
    qg_all[z] = qg_part[0] + qg_xh[...]
    z_back(0, whole, 0, 2)
    z_back(0, whole, 1, 6)
    z_back(0, whole, 2, 1)
    z_back(0, whole, 3, 7)
    for off in (1, 3, 2):
        s = along_y(off)
        take(kg_all.at[s], ka_rs.at[s])
        pass_on(s, across, 4 + off)
        pass_on(s, partner, 7 + off)
    z_take(6, whole, 0)
    z_back(6, front, 4, 2)
    z_back(6, whole, 5, 1)
    z_take(2, whole, 1)
    z_back(2, rear, 6, 6)
    z_back(2, whole, 7, 7)
    for off in (0, 1, 3, 2):
        s = (1 - x) * 8 + ((y + off) % 4) * 2 + core
        take(kg_all.at[s], ka_rs.at[s])
        pass_on(s, partner, 11 + off)

    z_take(7, whole, 2)
    z_take(1, whole, 3)
    z_take(4, front, 4)
    z_take(5, whole, 5)
    z_take(4, rear, 6)
    z_take(3, whole, 7)
    for c in range(8):
        s = c * 2 + (1 - core)
        take(kg_all.at[s], ka_rs.at[s])

    for b in range(8):
        take(stat_all.at[b], stat_ss.at[b])
        take(tc_ref.at[b], tc_ss.at[b])
        take(kc_ref.at[b], kc_ss.at[b])
    take(ist_all, ist_ss)
    for b in range(4):
        take(tx_ref.at[b], tx_ss.at[b])
        take(kx_ref.at[b], kx_ss.at[b])
    for j in range(3):
        take(ty_ref.at[j], ty_ss.at[j])
        take(ky_ref.at[j], ky_ss.at[j])
    take(qg_four.at[0:72], qg_ss.at[0])
    take(qg_four.at[72:136], qg_ss.at[1])
    for j in range(6):
        take(qg_recv.at[j], qg_ss.at[2 + j])
    for n, part in enumerate((whole, whole, whole, whole, front, whole, rear, whole)):
        take(qg_all.at[0, part], qa_ss.at[n])
    take(qg_xh, xh_ss)
    for n in range(15):
        take(kg_all.at[n], ka_ss.at[n])


def scoped(*refs):
    pl.run_scoped(
        functools.partial(fused, *refs),
        pltpu.VMEM((576, 2048), BF16),
        pltpu.VMEM((8, 8, 32, 576), BF16),
        pltpu.VMEM((2048, 2048), BF16),
        pltpu.VMEM((1024, 2048), BF16),
        pltpu.VMEM((128, 1024), BF16),
        pltpu.VMEM((2048, 128), BF16),
        pltpu.VMEM((16, 16, 2048), BF16),
        pltpu.VMEM((1024, 2048), BF16),
        pltpu.VMEM((128, 2048), BF16),
    )


def finish(qg_all, kg_all, qg_out, kg_out, wg_out):
    for i in range(8):
        qg_out[i * 128:(i + 1) * 128, :] = qg_all[i, 0:128, :]
        wg_out[i * 2:(i + 1) * 2, :] = qg_all[i, 128:130, 0:64]
    for i in range(16):
        kg_out[i * 128:(i + 1) * 128, :] = kg_all[i]


def shards(main_query, latent_keys, index_query, index_keys, index_weight, query_pos, kl_weight):
    vmem = pl.BlockSpec(memory_space=pltpu.VMEM)
    smem = pl.BlockSpec(memory_space=pltpu.SMEM)
    hbm = pl.BlockSpec(memory_space=pl.ANY)
    dma = pltpu.SemaphoreType.DMA
    query_blocks, key_blocks = pl.pallas_call(
        scoped,
        out_shape=(
            jax.ShapeDtypeStruct((8, 136, 128), F32),
            jax.ShapeDtypeStruct((16, 128, 128), F32),
        ),
        in_specs=[smem, smem, hbm, hbm, vmem, vmem, vmem],
        out_specs=(vmem, vmem),
        scratch_shapes=[
            pltpu.VMEM((8, 576, 256), BF16),
            pltpu.VMEM((576, 2048), BF16),
            pltpu.VMEM((32, 128), F32),
            pltpu.VMEM((256, 2048), F32),
            pltpu.VMEM((256, 2048), F32),
            pltpu.VMEM((256, 128), F32),
            pltpu.VMEM((8, 2, 256), F32),
            pltpu.VMEM((8, 15, 2, 256), F32),
            pltpu.VMEM((8, 2, 16, 2048), F32),
            pltpu.VMEM((8, 16, 2048), F32),
            pltpu.VMEM((4, 16, 2048), F32),
            pltpu.VMEM((3, 16, 2048), F32),
            pltpu.VMEM((128, 128), F32),
            pltpu.VMEM((1024, 128), F32),
            pltpu.VMEM((4, 8, 2048), F32),
            pltpu.VMEM((16, 2048), F32),
            pltpu.VMEM((16, 128), F32),
            pltpu.VMEM((15, 16, 128), F32),
            pltpu.VMEM((128, 128), F32),
            pltpu.VMEM((8, 136, 128), F32),
            pltpu.VMEM((6, 136, 128), F32),
            pltpu.VMEM((136, 128), F32),
            pltpu.VMEM((136, 128), F32),
            pltpu.VMEM((8, 2, 128, 128), F32),
            pltpu.VMEM((8, 128, 128), F32),
            pltpu.VMEM((4, 128, 128), F32),
            pltpu.VMEM((3, 128, 128), F32),
            dma((8,)), dma,
            dma((8,)), dma((8,)), dma, dma,
            dma((8,)), dma((8,)), dma((4,)), dma((4,)), dma((3,)), dma((3,)),
            dma((8,)), dma((8,)), dma, dma, dma((8,)), dma((8,)),
            dma((8,)), dma((8,)), dma((4,)), dma((4,)), dma((3,)), dma((3,)),
            dma((15,)), dma((16,)),
        ],
        compiler_params=pltpu.CompilerParams(
            collective_id=0, has_side_effects=True, vmem_limit_bytes=60 * 1024 * 1024
        ),
        name="fused_indexer_step",
    )(
        query_pos,
        kl_weight,
        jnp.transpose(main_query, (1, 2, 0)),
        jnp.transpose(latent_keys, (1, 0)),
        index_query.reshape(1024, 128),
        index_keys,
        index_weight,
    )
    query_grad, key_grad, weight_grad = pl.pallas_call(
        finish,
        out_shape=(
            jax.ShapeDtypeStruct((1024, 128), F32),
            jax.ShapeDtypeStruct((2048, 128), F32),
            jax.ShapeDtypeStruct((16, 64), F32),
        ),
        in_specs=[vmem, vmem],
        out_specs=(vmem, vmem, vmem),
        name="finish",
    )(query_blocks, key_blocks)
    return query_grad.reshape(16, 64, 128), key_grad, weight_grad


def solution(mesh):
    placed = (
        P(None, "heads", None),
        P("keys", None),
        P("heads", None, None),
        P("keys", None),
        P("heads", None),
        P(),
        P("heads"),
    )
    return jax.shard_map(
        shards,
        mesh=mesh,
        in_specs=placed,
        out_specs=(P("heads", None, None), P("keys", None), P("heads", None)),
        check_vma=False,
    )
```

```python
import functools

import jax
import jax.numpy as jnp
from jax import lax
from jax.experimental import pallas as pl
from jax.experimental.pallas import tpu as pltpu
from jax.sharding import PartitionSpec as P

H = 128
SCALE = 192.0 ** (-0.5)
SCALE2 = SCALE * 1.4426950408889634
MASKED = -1e30
FLOOR = -1e29
HUGE = 1e30
MESH = pl.DeviceIdType.MESH
LAG = 3
NT = (((1,), (1,)), ((), ()))
F32 = jnp.float32
BF16 = jnp.bfloat16


def lanes(t):
    return slice(t * 128, (t + 1) * 128)


def fused(
    pos_s, kl_s, mqt_hbm, lkt_hbm, iq, ik, iw,
    qg_hbm, kg_hbm,
    mqt, lkt_in, posb_ref,
    s_a, s_b, st_ref, stat_mine, stat_all,
    tp_ref, tc_ref, tx_ref, ty_ref,
    wpad_ref, wcol_ref, is_ref, ie_ref, ist_mine, ist_all,
    wgc_ref, qg_part, qg_recv, qg_four, qg_xh,
    kp_ref, kc_ref, kx_ref, ky_ref, qg_all, kg_all,
    mq_in, lk_in, qg_out, kg_out,
    stat_ss, stat_rs, ist_ss, ist_rs,
    tc_ss, tc_rs, tx_ss, tx_rs, ty_ss, ty_rs,
    qg_ss, qg_rs, xh_ss, xh_rs, qa_ss, qa_rs,
    kc_ss, kc_rs, kx_ss, kx_rs, ky_ss, ky_rs, ka_ss, ka_rs,
    lkt, mq_ref, e_ref, lg_ref, iqt_ref, ikc, d_ref, sl_ref, ikt,
):
    for i in range(8):
        pltpu.make_async_copy(mqt_hbm.at[i], mqt.at[i], mq_in.at[i]).start()
    pltpu.make_async_copy(lkt_hbm, lkt_in, lk_in).start()
    h = lax.axis_index("heads")
    k = lax.axis_index("keys")
    core, y, x = h % 2, (h // 2) % 4, h // 8
    z, xh = k // 2, k % 2
    key_first = k * 2048
    partner = x * 8 + y * 2 + (1 - core)
    across = (1 - x) * 8 + y * 2 + core

    def along_y(off):
        return x * 8 + ((y + off) % 4) * 2 + core

    def chip(b):
        return ((x + 1 - b // 4) % 2) * 4 + (y + 3 - b % 4) % 4

    barrier = pltpu.get_barrier_semaphore()
    for r in range(1, 16):
        pl.semaphore_signal(barrier, inc=1, device_id={"keys": (k + r) % 16}, device_id_type=MESH)
    for peer in (partner, across, along_y(1), along_y(2), along_y(3)):
        pl.semaphore_signal(barrier, inc=1, device_id={"heads": peer}, device_id_type=MESH)

    lane = lax.broadcasted_iota(jnp.int32, (1, 128), 1)
    sub = lax.broadcasted_iota(jnp.int32, (8, 128), 0)

    ikc[...] = ik[...]

    wpad_ref[...] = jnp.zeros((128, 128), F32)
    wpad_ref[0:16, 0:64] = iw[...]
    wturned = jnp.transpose(wpad_ref[...])
    for q in range(16):
        wcol_ref[q * 64:(q + 1) * 64, :] = jnp.broadcast_to(wturned[0:64, q:q + 1], (64, 128))
    def index_part(g, i):
        rows = pl.ds(pl.multiple_of(g * 256, 256), 256)
        got = lax.dot_general(
            iq[rows, :], ikc[pl.ds(pl.multiple_of(i * 256, 256), 256), :], NT, preferred_element_type=F32
        )
        for j in range(4):
            qrows = pl.ds(pl.multiple_of(g * 256 + j * 64, 64), 64)
            for t in range(2):
                cols = pl.ds(pl.multiple_of(i * 256 + t * 128, 128), 128)
                v = got[j * 64:(j + 1) * 64, lanes(t)]
                lg_ref[qrows, cols] = v.astype(BF16)
                is_ref[g, j:j + 1, cols] = jnp.sum(
                    jnp.maximum(v, 0.0) * wcol_ref[qrows, :], axis=0, keepdims=True
                )

    unit = lax.broadcasted_iota(jnp.int32, (256, 256), 0) == lax.broadcasted_iota(jnp.int32, (256, 256), 1)
    unit = jnp.where(unit, 1.0, 0.0).astype(BF16)

    def turn(i, carry):
        pltpu.make_async_copy(mqt_hbm.at[i], mqt.at[i], mq_in.at[i]).wait()
        got = lax.dot_general(unit, mqt[i], NT, preferred_element_type=F32).astype(BF16)
        for c in range(8):
            mq_ref[c, i] = got[c * 32:(c + 1) * 32, :]
        index_part(0, i)
        index_part(1, i)
        return carry

    lax.fori_loop(0, 8, turn, 0)
    pltpu.make_async_copy(lkt_hbm, lkt_in, lk_in).wait()

    def settle(i, carry):
        rows = pl.ds(pl.multiple_of(i * 64, 64), 64)
        lkt[rows, :] = lkt_in[rows, :]
        return carry

    lax.fori_loop(0, 9, settle, 0)

    def to_heads(src, dst, ss, rs, peer):
        return pltpu.make_async_remote_copy(
            src_ref=src, dst_ref=dst, send_sem=ss, recv_sem=rs,
            device_id={"heads": peer}, device_id_type=MESH,
        )

    def to_keys(src, dst, ss, rs, peer):
        return pltpu.make_async_remote_copy(
            src_ref=src, dst_ref=dst, send_sem=ss, recv_sem=rs,
            device_id={"keys": peer}, device_id_type=MESH,
        )

    def take(ref, sem):
        pltpu.make_async_copy(ref, ref, sem).wait()

    def score_quarter(b, i, s_ref):
        cols = pl.ds(pl.multiple_of(i * 512, 512), 512)
        s_ref[:, cols] = jnp.dot(
            mq_ref[chip(b)].reshape(256, 576), lkt[:, cols], preferred_element_type=F32
        )

    def soft_piece(b, i, s_ref):
        r0 = pl.multiple_of(chip(b) * 256, 256)
        rows = pl.ds(pl.multiple_of(i * 32, 32), 32)
        reach = posb_ref[...]
        top = jnp.full((32, 128), FLOOR, F32)
        for t in range(16):
            v = jnp.minimum(s_ref[rows, lanes(t)], reach + (0.5 - t * 128) * HUGE)
            s_ref[rows, lanes(t)] = v
            top = jnp.maximum(top, v)
        mcol = jnp.broadcast_to(jnp.max(top, axis=1, keepdims=True), (32, 128))
        total = jnp.zeros((32, 128), F32)
        erows = pl.ds(pl.multiple_of(r0 + i * 32, 32), 32)
        for t in range(16):
            e = jnp.exp2((s_ref[rows, lanes(t)] - mcol) * SCALE2)
            total = total + e
            e_ref[erows, lanes(t)] = e.astype(BF16)
        lcol = jnp.broadcast_to(jnp.sum(total, axis=1, keepdims=True), (32, 128))
        st_ref[rows, :] = jnp.where(lane == 0, mcol, lcol)

    def reach_of(b):
        for n in range(4):
            got = jnp.zeros((8, 128), jnp.int32)
            for j in range(8):
                got = jnp.where(sub == j, pos_s[chip(b) * 32 + n * 8 + j] - key_first, got)
            posb_ref[n * 8:(n + 1) * 8, :] = (got - lane).astype(F32) * HUGE

    def send_stats(b):
        stat_mine[b] = jnp.transpose(st_ref[...])[0:2, :]
        for r in range(1, 16):
            to_keys(stat_mine.at[b], stat_all.at[b, r - 1], stat_ss.at[b], stat_rs.at[b], (k + r) % 16).start()

    def target_block(b):
        take(stat_all.at[b], stat_rs.at[b])
        mine = stat_mine[b]
        m0, l0 = mine[0:1, :], mine[1:2, :]
        ms = [stat_all[b, r][0:1, :] for r in range(15)]
        ls = [stat_all[b, r][1:2, :] for r in range(15)]
        top = m0
        for m in ms:
            top = jnp.maximum(top, m)
        share = jnp.exp((m0 - top) * SCALE)
        total = l0 * share
        for m, l in zip(ms, ls):
            total = total + l * jnp.exp((m - top) * SCALE)
        w = share / (total * float(H))
        high = w.astype(BF16).astype(F32)
        low = w - high
        mine_of = lax.broadcasted_iota(jnp.int32, (32, 256), 1) % 32 == lax.broadcasted_iota(
            jnp.int32, (32, 256), 0
        )
        a = jnp.concatenate([jnp.where(mine_of, high, 0.0), jnp.where(mine_of, low, 0.0)], axis=0)
        r0 = pl.multiple_of(chip(b) * 256, 256)
        got = jnp.dot(a.astype(BF16), e_ref[pl.ds(r0, 256), :], preferred_element_type=F32)
        got = got[0:32, :] + got[32:64, :]
        tp_ref[b, 0] = got[0:16, :]
        tp_ref[b, 1] = got[16:32, :]
        to_heads(tp_ref.at[b, 1 - core], tc_ref.at[b], tc_ss.at[b], tc_rs.at[b], partner).start()

    def cross_x(b, p_ref, c_ref, x_ref, c_rs, x_ss, x_rs):
        take(c_ref.at[b], c_rs.at[b])
        p_ref[b, core] = p_ref[b, core] + c_ref[b]
        to_heads(p_ref.at[b, core], x_ref.at[b], x_ss.at[b], x_rs.at[b], across).start()

    def cross_y(i, p_ref, c_ref, x_ref, y_ref, c_rs, x_rs, y_ss, y_rs):
        b = 4 + i
        take(c_ref.at[b], c_rs.at[b])
        take(x_ref.at[i], x_rs.at[i])
        p_ref[b, core] = p_ref[b, core] + c_ref[b] + x_ref[i]
        off = 3 - i
        if off:
            to_heads(
                p_ref.at[b, core], y_ref.at[off - 1], y_ss.at[off - 1], y_rs.at[off - 1], along_y(off)
            ).start()

    def first(i, carry):
        score_quarter(0, i, s_a)
        for j in range(2):
            rows = pl.ds(pl.multiple_of(i * 256 + j * 128, 128), 128)
            iqt_ref[:, rows] = jnp.transpose(iq[rows, :].astype(F32) * wcol_ref[rows, :]).astype(BF16)
        return carry

    lax.fori_loop(0, 4, first, 0)
    pl.semaphore_wait(barrier, 20)

    def one_block(b, s_now, s_next):
        reach_of(b)

        for i in range(4):
            soft_piece(b, i * 2, s_now)
            score_quarter(jnp.minimum(b + 1, 7), i, s_next)
            soft_piece(b, i * 2 + 1, s_now)
        send_stats(b)

        @pl.when(b >= LAG)
        def _():
            target_block(b - LAG)

        @pl.when(b >= LAG + 1)
        def _():
            cross_x(b - LAG - 1, tp_ref, tc_ref, tx_ref, tc_rs, tx_ss, tx_rs)

    def two_blocks(n, carry):
        one_block(n * 2, s_a, s_b)
        one_block(n * 2 + 1, s_b, s_a)
        return carry

    lax.fori_loop(0, 4, two_blocks, 0)

    def own_chip(i):
        cross_y(i, tp_ref, tc_ref, tx_ref, ty_ref, tc_rs, tx_rs, ty_ss, ty_rs)

    target_block(5)

    def index_rest(i, carry):
        index_part(2, i)
        index_part(3, i)

        @pl.when(i == 4)
        def _():
            own_chip(0)

        return carry

    lax.fori_loop(0, 8, index_rest, 0)
    own_chip(1)

    row = lax.broadcasted_iota(jnp.int32, (16, 128), 0)
    posr = jnp.zeros((16, 128), jnp.int32)
    klr = jnp.zeros((16, 128), F32)
    for q in range(16):
        posr = jnp.where(row == q, pos_s[h * 16 + q] - key_first, posr)
        klr = jnp.where(row == q, kl_s[q], klr)
    top = jnp.full((16, 128), FLOOR, F32)
    for t in range(16):
        v = jnp.concatenate([is_ref[g, 0:4, lanes(t)] for g in range(4)], axis=0)
        v = jnp.where(lane + t * 128 <= posr, v, MASKED)
        ie_ref[:, lanes(t)] = v
        top = jnp.maximum(top, v)
    im = jnp.broadcast_to(jnp.max(top, axis=1, keepdims=True), (16, 128))
    total = jnp.zeros((16, 128), F32)
    for t in range(16):
        e = jnp.exp(ie_ref[:, lanes(t)] - im)
        total = total + e
        ie_ref[:, lanes(t)] = e
    il = jnp.broadcast_to(jnp.sum(total, axis=1, keepdims=True), (16, 128))
    ist_mine[...] = jnp.where(lane == 0, im, il)
    for r in range(1, 16):
        to_keys(ist_mine, ist_all.at[r - 1], ist_ss, ist_rs, (k + r) % 16).start()

    def turn_keys(i, carry):
        for j in range(4):
            rows = pl.ds(pl.multiple_of(i * 512 + j * 128, 128), 128)
            ikt[:, rows] = jnp.transpose(ik[rows, :].astype(F32)).astype(BF16)
        return carry

    lax.fori_loop(0, 4, turn_keys, 0)
    target_block(6)
    target_block(7)
    own_chip(2)
    own_chip(3)

    take(ist_all, ist_rs)
    ms = [jnp.broadcast_to(ist_all[r][:, 0:1], (16, 128)) for r in range(15)]
    top = im
    for m in ms:
        top = jnp.maximum(top, m)
    share = jnp.exp(im - top)
    total = il * share
    for r in range(15):
        total = total + jnp.broadcast_to(ist_all[r][:, 1:2], (16, 128)) * jnp.exp(ms[r] - top)
    share = share / total

    for j in range(3):
        take(ty_ref.at[j], ty_rs.at[j])
    for t in range(16):
        target = tp_ref[7, core, :, lanes(t)]
        for j in range(3):
            target = target + ty_ref[j, :, lanes(t)]
        delta = klr * (ie_ref[:, lanes(t)] * share - target)
        for q in range(16):
            d_ref[q, :, lanes(t)] = jnp.broadcast_to(delta[q:q + 1, :], (16, 128)).astype(BF16)

    def z_peer(off):
        return ((z + off) % 8) * 2 + xh

    def back_step(offsets):
        picked = []
        for off in offsets:
            q0 = ((z + off) % 8) * 2
            for j in range(2):
                qrows = pl.ds(pl.multiple_of((q0 + j) * 64, 64), 64)
                for t in range(16):
                    d = jnp.concatenate([d_ref[q0 + j, :, lanes(t)]] * 4, axis=0)
                    sl_ref[qrows, lanes(t)] = jnp.where(
                        lg_ref[qrows, lanes(t)] > 0, d, jnp.zeros((64, 128), BF16)
                    )
            picked.append(pl.ds(pl.multiple_of(q0 * 64, 128), 128))
        gate = jnp.concatenate([sl_ref[rows, :] for rows in picked], axis=0)
        both = jnp.transpose(lax.dot_general(ikt[...], gate, NT, preferred_element_type=F32))
        columns = jnp.zeros((64, 128), F32)
        for n, (off, rows) in enumerate(zip(offsets, picked)):
            got = both[n * 128:(n + 1) * 128, :]
            along = jnp.sum(got * iq[rows, :].astype(F32), axis=1, keepdims=True)
            for j in range(2):
                columns = jnp.where(
                    lane == n * 8 + j, jnp.broadcast_to(along[j * 64:(j + 1) * 64], (64, 128)), columns
                )
            qg_part[off, 0:128, :] = got * wcol_ref[rows, :]
        wgc_ref[0:64, :] = columns
        turned = jnp.transpose(wgc_ref[...])
        for n, off in enumerate(offsets):
            qg_part[off, 128:136, :] = turned[n * 8:(n + 1) * 8, :]

    def z_send(src, dst, n, off):
        to_keys(src, dst, qg_ss.at[n], qg_rs.at[n], z_peer(off)).start()

    wgc_ref[...] = jnp.zeros((128, 128), F32)
    back_step((4, 3))
    z_send(qg_part.at[4, 0:72], qg_four.at[0:72], 0, 2)
    z_send(qg_part.at[4, 72:136], qg_four.at[72:136], 1, 6)
    z_send(qg_part.at[3], qg_recv.at[0], 2, 1)
    back_step((5, 2))
    z_send(qg_part.at[5], qg_recv.at[1], 3, 7)
    back_step((6, 1))
    z_send(qg_part.at[1], qg_recv.at[2], 4, 1)
    back_step((7, 0))
    z_send(qg_part.at[7], qg_recv.at[3], 5, 7)

    def z_join():
        take(qg_recv.at[0], qg_rs.at[2])
        take(qg_four.at[0:72], qg_rs.at[0])
        qg_part[2, 0:72, :] = qg_part[2, 0:72, :] + qg_recv[0, 0:72, :] + qg_four[0:72, :]
        qg_part[2, 72:136, :] = qg_part[2, 72:136, :] + qg_recv[0, 72:136, :]
        z_send(qg_part.at[2], qg_recv.at[4], 6, 2)
        take(qg_recv.at[1], qg_rs.at[3])
        take(qg_four.at[72:136], qg_rs.at[1])
        qg_part[6, 0:72, :] = qg_part[6, 0:72, :] + qg_recv[1, 0:72, :]
        qg_part[6, 72:136, :] = qg_part[6, 72:136, :] + qg_recv[1, 72:136, :] + qg_four[72:136, :]
        z_send(qg_part.at[6], qg_recv.at[5], 7, 6)

    def key_step(b, carry):
        cols = pl.ds(pl.multiple_of(chip(b) * 256, 256), 256)
        got = jnp.dot(iqt_ref[...], sl_ref[:, cols], preferred_element_type=F32)
        kp_ref[b, 0] = got[:, 0:128]
        kp_ref[b, 1] = got[:, 128:256]
        to_heads(kp_ref.at[b, 1 - core], kc_ref.at[b], kc_ss.at[b], kc_rs.at[b], partner).start()

        @pl.when(b >= 4)
        def _():
            cross_x(b - 4, kp_ref, kc_ref, kx_ref, kc_rs, kx_ss, kx_rs)

        return carry

    lax.fori_loop(0, 8, key_step, 0)
    z_join()

    def key_chip(i):
        cross_y(i, kp_ref, kc_ref, kx_ref, ky_ref, kc_rs, kx_rs, ky_ss, ky_rs)

    for i in range(3):
        key_chip(i)

    for j in range(4):
        take(qg_recv.at[2 + j], qg_rs.at[4 + j])
    qg_part[0] = qg_part[0] + (qg_recv[2] + qg_recv[3]) + (qg_recv[4] + qg_recv[5])
    to_keys(qg_part.at[0], qg_xh, xh_ss, xh_rs, z * 2 + (1 - xh)).start()

    key_chip(3)

    for j in range(3):
        take(ky_ref.at[j], ky_rs.at[j])
    shard = kp_ref[7, core]
    for j in range(3):
        shard = shard + ky_ref[j]
    kg_all[h] = jnp.transpose(shard)

    def key_done(s):
        pltpu.make_async_copy(kg_all.at[s], kg_hbm.at[s], kg_out.at[s]).start()

    def query_done(off):
        i = (z + off) % 8
        pltpu.make_async_copy(qg_all.at[i], qg_hbm.at[i], qg_out.at[i]).start()

    def pass_on(s, peer, n):
        to_heads(kg_all.at[s], kg_all.at[s], ka_ss.at[n], ka_rs.at[s], peer).start()

    for off in (1, 2, 3):
        pass_on(h, along_y(off), off - 1)
    pass_on(h, across, 3)
    pass_on(h, partner, 4)

    def z_back(off_from, part, n, off):
        ref = qg_all.at[(z + off_from) % 8, part]
        to_keys(ref, ref, qa_ss.at[n], qa_rs.at[n], z_peer(off)).start()

    def z_take(off_from, part, n):
        take(qg_all.at[(z + off_from) % 8, part], qa_rs.at[n])

    whole, front, rear = slice(0, 136), slice(0, 72), slice(72, 136)
    take(qg_xh, xh_rs)
    qg_all[z] = qg_part[0] + qg_xh[...]
    z_back(0, whole, 0, 2)
    z_back(0, whole, 1, 6)
    z_back(0, whole, 2, 1)
    z_back(0, whole, 3, 7)
    for off in (1, 3, 2):
        s = along_y(off)
        take(kg_all.at[s], ka_rs.at[s])
        pass_on(s, across, 4 + off)
        pass_on(s, partner, 7 + off)
    z_take(6, whole, 0)
    z_back(6, front, 4, 2)
    z_back(6, whole, 5, 1)
    z_take(2, whole, 1)
    z_back(2, rear, 6, 6)
    z_back(2, whole, 7, 7)
    for off in (0, 1, 3, 2):
        s = (1 - x) * 8 + ((y + off) % 4) * 2 + core
        take(kg_all.at[s], ka_rs.at[s])
        pass_on(s, partner, 11 + off)

    key_done(h)
    for off in (1, 3, 2):
        key_done(along_y(off))
    for off in (0, 1, 3, 2):
        key_done((1 - x) * 8 + ((y + off) % 4) * 2 + core)
    z_take(7, whole, 2)
    z_take(1, whole, 3)
    for off in (0, 1, 2, 6, 7):
        query_done(off)
    for c in range(8):
        s = c * 2 + (1 - core)
        take(kg_all.at[s], ka_rs.at[s])
        key_done(s)
    z_take(4, front, 4)
    z_take(4, rear, 6)
    query_done(4)
    z_take(5, whole, 5)
    query_done(5)
    z_take(3, whole, 7)
    query_done(3)

    for b in range(8):
        take(stat_all.at[b], stat_ss.at[b])
        take(tc_ref.at[b], tc_ss.at[b])
        take(kc_ref.at[b], kc_ss.at[b])
    take(ist_all, ist_ss)
    for b in range(4):
        take(tx_ref.at[b], tx_ss.at[b])
        take(kx_ref.at[b], kx_ss.at[b])
    for j in range(3):
        take(ty_ref.at[j], ty_ss.at[j])
        take(ky_ref.at[j], ky_ss.at[j])
    take(qg_four.at[0:72], qg_ss.at[0])
    take(qg_four.at[72:136], qg_ss.at[1])
    for j in range(6):
        take(qg_recv.at[j], qg_ss.at[2 + j])
    for n, part in enumerate((whole, whole, whole, whole, front, whole, rear, whole)):
        take(qg_all.at[0, part], qa_ss.at[n])
    take(qg_xh, xh_ss)
    for n in range(15):
        take(kg_all.at[n], ka_ss.at[n])
    for i in range(8):
        pltpu.make_async_copy(qg_all.at[i], qg_hbm.at[i], qg_out.at[i]).wait()
    for i in range(16):
        pltpu.make_async_copy(kg_all.at[i], kg_hbm.at[i], kg_out.at[i]).wait()


def scoped(*refs):
    pl.run_scoped(
        functools.partial(fused, *refs),
        pltpu.VMEM((576, 2048), BF16),
        pltpu.VMEM((8, 8, 32, 576), BF16),
        pltpu.VMEM((2048, 2048), BF16),
        pltpu.VMEM((1024, 2048), BF16),
        pltpu.VMEM((128, 1024), BF16),
        pltpu.VMEM((2048, 128), BF16),
        pltpu.VMEM((16, 16, 2048), BF16),
        pltpu.VMEM((1024, 2048), BF16),
        pltpu.VMEM((128, 2048), BF16),
    )


def finish(qg_hbm, kg_hbm, qg_out, kg_out, wg_out, qg, kg, q_in, k_in, q_to, k_to):
    qs = [pltpu.make_async_copy(qg_hbm.at[pl.ds(i * 4, 4)], qg.at[pl.ds(i * 4, 4)], q_in.at[i]) for i in range(2)]
    ks = [pltpu.make_async_copy(kg_hbm.at[pl.ds(i * 4, 4)], kg.at[pl.ds(i * 4, 4)], k_in.at[i]) for i in range(4)]
    for copy in qs + ks:
        copy.start()
    outs = []
    for i in range(2):
        qs[i].wait()
        for j in range(i * 4, i * 4 + 4):
            outs.append(pltpu.make_async_copy(qg.at[j, pl.ds(0, 128)], qg_out.at[j], q_to.at[j]))
            outs[-1].start()
    for i in range(4):
        ks[i].wait()
        outs.append(pltpu.make_async_copy(kg.at[pl.ds(i * 4, 4)], kg_out.at[pl.ds(i * 4, 4)], k_to.at[i]))
        outs[-1].start()
    for i in range(8):
        wg_out[i * 2:(i + 1) * 2, :] = qg[i, 128:130, 0:64]
    for copy in outs:
        copy.wait()


def shards(main_query, latent_keys, index_query, index_keys, index_weight, query_pos, kl_weight):
    vmem = pl.BlockSpec(memory_space=pltpu.VMEM)
    smem = pl.BlockSpec(memory_space=pltpu.SMEM)
    hbm = pl.BlockSpec(memory_space=pl.ANY)
    dma = pltpu.SemaphoreType.DMA
    query_blocks, key_blocks = pl.pallas_call(
        scoped,
        out_shape=(
            jax.ShapeDtypeStruct((8, 136, 128), F32),
            jax.ShapeDtypeStruct((16, 128, 128), F32),
        ),
        in_specs=[smem, smem, hbm, hbm, vmem, vmem, vmem],
        out_specs=(hbm, hbm),
        scratch_shapes=[
            pltpu.VMEM((8, 576, 256), BF16),
            pltpu.VMEM((576, 2048), BF16),
            pltpu.VMEM((32, 128), F32),
            pltpu.VMEM((256, 2048), F32),
            pltpu.VMEM((256, 2048), F32),
            pltpu.VMEM((256, 128), F32),
            pltpu.VMEM((8, 2, 256), F32),
            pltpu.VMEM((8, 15, 2, 256), F32),
            pltpu.VMEM((8, 2, 16, 2048), F32),
            pltpu.VMEM((8, 16, 2048), F32),
            pltpu.VMEM((4, 16, 2048), F32),
            pltpu.VMEM((3, 16, 2048), F32),
            pltpu.VMEM((128, 128), F32),
            pltpu.VMEM((1024, 128), F32),
            pltpu.VMEM((4, 8, 2048), F32),
            pltpu.VMEM((16, 2048), F32),
            pltpu.VMEM((16, 128), F32),
            pltpu.VMEM((15, 16, 128), F32),
            pltpu.VMEM((128, 128), F32),
            pltpu.VMEM((8, 136, 128), F32),
            pltpu.VMEM((6, 136, 128), F32),
            pltpu.VMEM((136, 128), F32),
            pltpu.VMEM((136, 128), F32),
            pltpu.VMEM((8, 2, 128, 128), F32),
            pltpu.VMEM((8, 128, 128), F32),
            pltpu.VMEM((4, 128, 128), F32),
            pltpu.VMEM((3, 128, 128), F32),
            pltpu.VMEM((8, 136, 128), F32),
            pltpu.VMEM((16, 128, 128), F32),
            dma((8,)), dma, dma((8,)), dma((16,)),
            dma((8,)), dma((8,)), dma, dma,
            dma((8,)), dma((8,)), dma((4,)), dma((4,)), dma((3,)), dma((3,)),
            dma((8,)), dma((8,)), dma, dma, dma((8,)), dma((8,)),
            dma((8,)), dma((8,)), dma((4,)), dma((4,)), dma((3,)), dma((3,)),
            dma((15,)), dma((16,)),
        ],
        compiler_params=pltpu.CompilerParams(
            collective_id=0, has_side_effects=True, vmem_limit_bytes=60 * 1024 * 1024
        ),
        name="fused_indexer_step",
    )(
        query_pos,
        kl_weight,
        jnp.transpose(main_query, (1, 2, 0)),
        jnp.transpose(latent_keys, (1, 0)),
        index_query.reshape(1024, 128),
        index_keys,
        index_weight,
    )
    query_grad, key_grad, weight_grad = pl.pallas_call(
        finish,
        out_shape=(
            jax.ShapeDtypeStruct((8, 128, 128), F32),
            jax.ShapeDtypeStruct((16, 128, 128), F32),
            jax.ShapeDtypeStruct((16, 64), F32),
        ),
        in_specs=[hbm, hbm],
        out_specs=(hbm, hbm, vmem),
        scratch_shapes=[
            pltpu.VMEM((8, 136, 128), F32),
            pltpu.VMEM((16, 128, 128), F32),
            dma((2,)), dma((4,)), dma((8,)), dma((4,)),
        ],
        name="finish",
    )(query_blocks, key_blocks)
    return query_grad.reshape(16, 64, 128), key_grad.reshape(2048, 128), weight_grad


def solution(mesh):
    placed = (
        P(None, "heads", None),
        P("keys", None),
        P("heads", None, None),
        P("keys", None),
        P("heads", None),
        P(),
        P("heads"),
    )
    return jax.shard_map(
        shards,
        mesh=mesh,
        in_specs=placed,
        out_specs=(P("heads", None, None), P("keys", None), P("heads", None)),
        check_vma=False,
    )
```

```python
import functools

import jax
import jax.numpy as jnp
from jax import lax
from jax.experimental import pallas as pl
from jax.experimental.pallas import tpu as pltpu
from jax.sharding import PartitionSpec as P

H = 128
SCALE = 192.0 ** (-0.5)
SCALE2 = SCALE * 1.4426950408889634
MASKED = -1e30
FLOOR = -1e29
HUGE = 1e30
MESH = pl.DeviceIdType.MESH
LAG = 3
NT = (((1,), (1,)), ((), ()))
F32 = jnp.float32
BF16 = jnp.bfloat16


def lanes(t):
    return slice(t * 128, (t + 1) * 128)


def fused(
    pos_s, kl_s, mqt_hbm, lkt_hbm, iq, ik, iw,
    qg_all, kg_all,
    mqt, lkt_in, posb_ref,
    s_a, s_b, st_ref, stat_mine, stat_all,
    tp_ref, tc_ref, tx_ref, ty_ref,
    wpad_ref, wcol_ref, is_ref, ie_ref, ist_mine, ist_all,
    wgc_ref, qg_part, qg_recv, qg_four, qg_xh,
    kp_ref, kc_ref, kx_ref, ky_ref,
    mq_in, lk_in,
    stat_ss, stat_rs, ist_ss, ist_rs,
    tc_ss, tc_rs, tx_ss, tx_rs, ty_ss, ty_rs,
    qg_ss, qg_rs, xh_ss, xh_rs, qa_ss, qa_rs,
    kc_ss, kc_rs, kx_ss, kx_rs, ky_ss, ky_rs, ka_ss, ka_rs,
    lkt, mq_ref, e_ref, lg_ref, iqt_ref, ikc, d_ref, sl_ref, ikt,
):
    for i in range(8):
        pltpu.make_async_copy(mqt_hbm.at[i], mqt.at[i], mq_in.at[i]).start()
    pltpu.make_async_copy(lkt_hbm, lkt_in, lk_in).start()
    h = lax.axis_index("heads")
    k = lax.axis_index("keys")
    core, y, x = h % 2, (h // 2) % 4, h // 8
    z, xh = k // 2, k % 2
    key_first = k * 2048
    partner = x * 8 + y * 2 + (1 - core)
    across = (1 - x) * 8 + y * 2 + core

    def along_y(off):
        return x * 8 + ((y + off) % 4) * 2 + core

    def chip(b):
        return ((x + 1 - b // 4) % 2) * 4 + (y + 3 - b % 4) % 4

    barrier = pltpu.get_barrier_semaphore()
    for r in range(1, 16):
        pl.semaphore_signal(barrier, inc=1, device_id={"keys": (k + r) % 16}, device_id_type=MESH)
    for peer in (partner, across, along_y(1), along_y(2), along_y(3)):
        pl.semaphore_signal(barrier, inc=1, device_id={"heads": peer}, device_id_type=MESH)

    lane = lax.broadcasted_iota(jnp.int32, (1, 128), 1)
    sub = lax.broadcasted_iota(jnp.int32, (8, 128), 0)

    ikc[...] = ik[...]

    wpad_ref[...] = jnp.zeros((128, 128), F32)
    wpad_ref[0:16, 0:64] = iw[...]
    wturned = jnp.transpose(wpad_ref[...])
    for q in range(16):
        wcol_ref[q * 64:(q + 1) * 64, :] = jnp.broadcast_to(wturned[0:64, q:q + 1], (64, 128))
    def index_part(g, i):
        rows = pl.ds(pl.multiple_of(g * 256, 256), 256)
        got = lax.dot_general(
            iq[rows, :], ikc[pl.ds(pl.multiple_of(i * 256, 256), 256), :], NT, preferred_element_type=F32
        )
        for j in range(4):
            qrows = pl.ds(pl.multiple_of(g * 256 + j * 64, 64), 64)
            for t in range(2):
                cols = pl.ds(pl.multiple_of(i * 256 + t * 128, 128), 128)
                v = got[j * 64:(j + 1) * 64, lanes(t)]
                lg_ref[qrows, cols] = v.astype(BF16)
                is_ref[g, j:j + 1, cols] = jnp.sum(
                    jnp.maximum(v, 0.0) * wcol_ref[qrows, :], axis=0, keepdims=True
                )

    unit = lax.broadcasted_iota(jnp.int32, (256, 256), 0) == lax.broadcasted_iota(jnp.int32, (256, 256), 1)
    unit = jnp.where(unit, 1.0, 0.0).astype(BF16)

    def turn(i, carry):
        pltpu.make_async_copy(mqt_hbm.at[i], mqt.at[i], mq_in.at[i]).wait()
        got = lax.dot_general(unit, mqt[i], NT, preferred_element_type=F32).astype(BF16)
        for c in range(8):
            mq_ref[c, i] = got[c * 32:(c + 1) * 32, :]
        index_part(0, i)
        index_part(1, i)
        return carry

    lax.fori_loop(0, 8, turn, 0)
    pltpu.make_async_copy(lkt_hbm, lkt_in, lk_in).wait()

    def settle(i, carry):
        rows = pl.ds(pl.multiple_of(i * 64, 64), 64)
        lkt[rows, :] = lkt_in[rows, :]
        return carry

    lax.fori_loop(0, 9, settle, 0)

    def to_heads(src, dst, ss, rs, peer):
        return pltpu.make_async_remote_copy(
            src_ref=src, dst_ref=dst, send_sem=ss, recv_sem=rs,
            device_id={"heads": peer}, device_id_type=MESH,
        )

    def to_keys(src, dst, ss, rs, peer):
        return pltpu.make_async_remote_copy(
            src_ref=src, dst_ref=dst, send_sem=ss, recv_sem=rs,
            device_id={"keys": peer}, device_id_type=MESH,
        )

    def take(ref, sem):
        pltpu.make_async_copy(ref, ref, sem).wait()

    def score_quarter(b, i, s_ref):
        cols = pl.ds(pl.multiple_of(i * 512, 512), 512)
        s_ref[:, cols] = jnp.dot(
            mq_ref[chip(b)].reshape(256, 576), lkt[:, cols], preferred_element_type=F32
        )

    def soft_piece(b, i, s_ref):
        r0 = pl.multiple_of(chip(b) * 256, 256)
        rows = pl.ds(pl.multiple_of(i * 32, 32), 32)
        reach = posb_ref[...]
        top = jnp.full((32, 128), FLOOR, F32)
        for t in range(16):
            v = jnp.minimum(s_ref[rows, lanes(t)], reach + (0.5 - t * 128) * HUGE)
            s_ref[rows, lanes(t)] = v
            top = jnp.maximum(top, v)
        mcol = jnp.broadcast_to(jnp.max(top, axis=1, keepdims=True), (32, 128))
        total = jnp.zeros((32, 128), F32)
        erows = pl.ds(pl.multiple_of(r0 + i * 32, 32), 32)
        for t in range(16):
            e = jnp.exp2((s_ref[rows, lanes(t)] - mcol) * SCALE2)
            total = total + e
            e_ref[erows, lanes(t)] = e.astype(BF16)
        lcol = jnp.broadcast_to(jnp.sum(total, axis=1, keepdims=True), (32, 128))
        st_ref[rows, :] = jnp.where(lane == 0, mcol, lcol)

    def reach_of(b):
        for n in range(4):
            got = jnp.zeros((8, 128), jnp.int32)
            for j in range(8):
                got = jnp.where(sub == j, pos_s[chip(b) * 32 + n * 8 + j] - key_first, got)
            posb_ref[n * 8:(n + 1) * 8, :] = (got - lane).astype(F32) * HUGE

    def send_stats(b):
        stat_mine[b] = jnp.transpose(st_ref[...])[0:2, :]
        for r in range(1, 16):
            to_keys(stat_mine.at[b], stat_all.at[b, r - 1], stat_ss.at[b], stat_rs.at[b], (k + r) % 16).start()

    def target_block(b):
        take(stat_all.at[b], stat_rs.at[b])
        mine = stat_mine[b]
        m0, l0 = mine[0:1, :], mine[1:2, :]
        ms = [stat_all[b, r][0:1, :] for r in range(15)]
        ls = [stat_all[b, r][1:2, :] for r in range(15)]
        top = m0
        for m in ms:
            top = jnp.maximum(top, m)
        share = jnp.exp((m0 - top) * SCALE)
        total = l0 * share
        for m, l in zip(ms, ls):
            total = total + l * jnp.exp((m - top) * SCALE)
        w = share / (total * float(H))
        high = w.astype(BF16).astype(F32)
        low = w - high
        mine_of = lax.broadcasted_iota(jnp.int32, (32, 256), 1) % 32 == lax.broadcasted_iota(
            jnp.int32, (32, 256), 0
        )
        a = jnp.concatenate([jnp.where(mine_of, high, 0.0), jnp.where(mine_of, low, 0.0)], axis=0)
        r0 = pl.multiple_of(chip(b) * 256, 256)
        got = jnp.dot(a.astype(BF16), e_ref[pl.ds(r0, 256), :], preferred_element_type=F32)
        got = got[0:32, :] + got[32:64, :]
        tp_ref[b, 0] = got[0:16, :]
        tp_ref[b, 1] = got[16:32, :]
        to_heads(tp_ref.at[b, 1 - core], tc_ref.at[b], tc_ss.at[b], tc_rs.at[b], partner).start()

    def cross_x(b, p_ref, c_ref, x_ref, c_rs, x_ss, x_rs):
        take(c_ref.at[b], c_rs.at[b])
        p_ref[b, core] = p_ref[b, core] + c_ref[b]
        to_heads(p_ref.at[b, core], x_ref.at[b], x_ss.at[b], x_rs.at[b], across).start()

    def cross_y(i, p_ref, c_ref, x_ref, y_ref, c_rs, x_rs, y_ss, y_rs):
        b = 4 + i
        take(c_ref.at[b], c_rs.at[b])
        take(x_ref.at[i], x_rs.at[i])
        p_ref[b, core] = p_ref[b, core] + c_ref[b] + x_ref[i]
        off = 3 - i
        if off:
            to_heads(
                p_ref.at[b, core], y_ref.at[off - 1], y_ss.at[off - 1], y_rs.at[off - 1], along_y(off)
            ).start()

    def first(i, carry):
        score_quarter(0, i, s_a)
        for j in range(2):
            rows = pl.ds(pl.multiple_of(i * 256 + j * 128, 128), 128)
            iqt_ref[:, rows] = jnp.transpose(iq[rows, :].astype(F32) * wcol_ref[rows, :]).astype(BF16)
        return carry

    lax.fori_loop(0, 4, first, 0)
    pl.semaphore_wait(barrier, 20)

    def one_block(b, s_now, s_next):
        reach_of(b)

        for i in range(4):
            soft_piece(b, i * 2, s_now)
            score_quarter(jnp.minimum(b + 1, 7), i, s_next)
            soft_piece(b, i * 2 + 1, s_now)
        send_stats(b)

        @pl.when(b >= LAG)
        def _():
            target_block(b - LAG)

        @pl.when(b >= LAG + 1)
        def _():
            cross_x(b - LAG - 1, tp_ref, tc_ref, tx_ref, tc_rs, tx_ss, tx_rs)

    def two_blocks(n, carry):
        one_block(n * 2, s_a, s_b)
        one_block(n * 2 + 1, s_b, s_a)
        return carry

    lax.fori_loop(0, 4, two_blocks, 0)

    def own_chip(i):
        cross_y(i, tp_ref, tc_ref, tx_ref, ty_ref, tc_rs, tx_rs, ty_ss, ty_rs)

    target_block(5)

    def index_rest(i, carry):
        index_part(2, i)
        index_part(3, i)

        @pl.when(i == 4)
        def _():
            own_chip(0)

        return carry

    lax.fori_loop(0, 8, index_rest, 0)
    own_chip(1)

    row = lax.broadcasted_iota(jnp.int32, (16, 128), 0)
    posr = jnp.zeros((16, 128), jnp.int32)
    klr = jnp.zeros((16, 128), F32)
    for q in range(16):
        posr = jnp.where(row == q, pos_s[h * 16 + q] - key_first, posr)
        klr = jnp.where(row == q, kl_s[q], klr)
    top = jnp.full((16, 128), FLOOR, F32)
    for t in range(16):
        v = jnp.concatenate([is_ref[g, 0:4, lanes(t)] for g in range(4)], axis=0)
        v = jnp.where(lane + t * 128 <= posr, v, MASKED)
        ie_ref[:, lanes(t)] = v
        top = jnp.maximum(top, v)
    im = jnp.broadcast_to(jnp.max(top, axis=1, keepdims=True), (16, 128))
    total = jnp.zeros((16, 128), F32)
    for t in range(16):
        e = jnp.exp(ie_ref[:, lanes(t)] - im)
        total = total + e
        ie_ref[:, lanes(t)] = e
    il = jnp.broadcast_to(jnp.sum(total, axis=1, keepdims=True), (16, 128))
    ist_mine[...] = jnp.where(lane == 0, im, il)
    for r in range(1, 16):
        to_keys(ist_mine, ist_all.at[r - 1], ist_ss, ist_rs, (k + r) % 16).start()

    def turn_keys(i, carry):
        for j in range(4):
            rows = pl.ds(pl.multiple_of(i * 512 + j * 128, 128), 128)
            ikt[:, rows] = jnp.transpose(ik[rows, :].astype(F32)).astype(BF16)
        return carry

    lax.fori_loop(0, 4, turn_keys, 0)
    target_block(6)
    target_block(7)
    own_chip(2)
    own_chip(3)

    take(ist_all, ist_rs)
    ms = [jnp.broadcast_to(ist_all[r][:, 0:1], (16, 128)) for r in range(15)]
    top = im
    for m in ms:
        top = jnp.maximum(top, m)
    share = jnp.exp(im - top)
    total = il * share
    for r in range(15):
        total = total + jnp.broadcast_to(ist_all[r][:, 1:2], (16, 128)) * jnp.exp(ms[r] - top)
    share = share / total

    for j in range(3):
        take(ty_ref.at[j], ty_rs.at[j])
    for t in range(16):
        target = tp_ref[7, core, :, lanes(t)]
        for j in range(3):
            target = target + ty_ref[j, :, lanes(t)]
        delta = klr * (ie_ref[:, lanes(t)] * share - target)
        for q in range(16):
            d_ref[q, :, lanes(t)] = jnp.broadcast_to(delta[q:q + 1, :], (16, 128)).astype(BF16)

    def z_peer(off):
        return ((z + off) % 8) * 2 + xh

    def back_step(offsets):
        picked = []
        for off in offsets:
            q0 = ((z + off) % 8) * 2
            for j in range(2):
                qrows = pl.ds(pl.multiple_of((q0 + j) * 64, 64), 64)
                for t in range(16):
                    d = jnp.concatenate([d_ref[q0 + j, :, lanes(t)]] * 4, axis=0)
                    sl_ref[qrows, lanes(t)] = jnp.where(
                        lg_ref[qrows, lanes(t)] > 0, d, jnp.zeros((64, 128), BF16)
                    )
            picked.append(pl.ds(pl.multiple_of(q0 * 64, 128), 128))
        gate = jnp.concatenate([sl_ref[rows, :] for rows in picked], axis=0)
        both = jnp.transpose(lax.dot_general(ikt[...], gate, NT, preferred_element_type=F32))
        columns = jnp.zeros((64, 128), F32)
        for n, (off, rows) in enumerate(zip(offsets, picked)):
            got = both[n * 128:(n + 1) * 128, :]
            along = jnp.sum(got * iq[rows, :].astype(F32), axis=1, keepdims=True)
            for j in range(2):
                columns = jnp.where(
                    lane == n * 8 + j, jnp.broadcast_to(along[j * 64:(j + 1) * 64], (64, 128)), columns
                )
            qg_part[off, 0:128, :] = got * wcol_ref[rows, :]
        wgc_ref[0:64, :] = columns
        turned = jnp.transpose(wgc_ref[...])
        for n, off in enumerate(offsets):
            qg_part[off, 128:136, :] = turned[n * 8:(n + 1) * 8, :]

    def z_send(src, dst, n, off):
        to_keys(src, dst, qg_ss.at[n], qg_rs.at[n], z_peer(off)).start()

    wgc_ref[...] = jnp.zeros((128, 128), F32)
    back_step((4, 3))
    z_send(qg_part.at[4, 0:72], qg_four.at[0:72], 0, 2)
    z_send(qg_part.at[4, 72:136], qg_four.at[72:136], 1, 6)
    z_send(qg_part.at[3], qg_recv.at[0], 2, 1)
    back_step((5, 2))
    z_send(qg_part.at[5], qg_recv.at[1], 3, 7)
    back_step((6, 1))
    z_send(qg_part.at[1], qg_recv.at[2], 4, 1)
    back_step((7, 0))
    z_send(qg_part.at[7], qg_recv.at[3], 5, 7)

    def z_join():
        take(qg_recv.at[0], qg_rs.at[2])
        take(qg_four.at[0:72], qg_rs.at[0])
        qg_part[2, 0:72, :] = qg_part[2, 0:72, :] + qg_recv[0, 0:72, :] + qg_four[0:72, :]
        qg_part[2, 72:136, :] = qg_part[2, 72:136, :] + qg_recv[0, 72:136, :]
        z_send(qg_part.at[2], qg_recv.at[4], 6, 2)
        take(qg_recv.at[1], qg_rs.at[3])
        take(qg_four.at[72:136], qg_rs.at[1])
        qg_part[6, 0:72, :] = qg_part[6, 0:72, :] + qg_recv[1, 0:72, :]
        qg_part[6, 72:136, :] = qg_part[6, 72:136, :] + qg_recv[1, 72:136, :] + qg_four[72:136, :]
        z_send(qg_part.at[6], qg_recv.at[5], 7, 6)

    def key_step(b, carry):
        cols = pl.ds(pl.multiple_of(chip(b) * 256, 256), 256)
        got = jnp.dot(iqt_ref[...], sl_ref[:, cols], preferred_element_type=F32)
        kp_ref[b, 0] = got[:, 0:128]
        kp_ref[b, 1] = got[:, 128:256]
        to_heads(kp_ref.at[b, 1 - core], kc_ref.at[b], kc_ss.at[b], kc_rs.at[b], partner).start()

        @pl.when(b >= 4)
        def _():
            cross_x(b - 4, kp_ref, kc_ref, kx_ref, kc_rs, kx_ss, kx_rs)

        return carry

    lax.fori_loop(0, 8, key_step, 0)
    z_join()

    def key_chip(i):
        cross_y(i, kp_ref, kc_ref, kx_ref, ky_ref, kc_rs, kx_rs, ky_ss, ky_rs)

    for i in range(3):
        key_chip(i)

    for j in range(4):
        take(qg_recv.at[2 + j], qg_rs.at[4 + j])
    qg_part[0] = qg_part[0] + (qg_recv[2] + qg_recv[3]) + (qg_recv[4] + qg_recv[5])
    to_keys(qg_part.at[0], qg_xh, xh_ss, xh_rs, z * 2 + (1 - xh)).start()

    key_chip(3)

    for j in range(3):
        take(ky_ref.at[j], ky_rs.at[j])
    shard = kp_ref[7, core]
    for j in range(3):
        shard = shard + ky_ref[j]
    kg_all[h] = jnp.transpose(shard)

    def pass_on(s, peer, n):
        to_heads(kg_all.at[s], kg_all.at[s], ka_ss.at[n], ka_rs.at[s], peer).start()

    for off in (1, 2, 3):
        pass_on(h, along_y(off), off - 1)
    pass_on(h, across, 3)
    pass_on(h, partner, 4)

    def z_back(off_from, part, n, off):
        ref = qg_all.at[(z + off_from) % 8, part]
        to_keys(ref, ref, qa_ss.at[n], qa_rs.at[n], z_peer(off)).start()

    def z_take(off_from, part, n):
        take(qg_all.at[(z + off_from) % 8, part], qa_rs.at[n])

    whole, front, rear = slice(0, 136), slice(0, 72), slice(72, 136)
    take(qg_xh, xh_rs)
    qg_all[z] = qg_part[0] + qg_xh[...]
    z_back(0, whole, 0, 2)
    z_back(0, whole, 1, 6)
    z_back(0, whole, 2, 1)
    z_back(0, whole, 3, 7)
    for off in (1, 3, 2):
        s = along_y(off)
        take(kg_all.at[s], ka_rs.at[s])
        pass_on(s, across, 4 + off)
        pass_on(s, partner, 7 + off)
    z_take(6, whole, 0)
    z_back(6, front, 4, 2)
    z_back(6, whole, 5, 1)
    z_take(2, whole, 1)
    z_back(2, rear, 6, 6)
    z_back(2, whole, 7, 7)
    for off in (0, 1, 3, 2):
        s = (1 - x) * 8 + ((y + off) % 4) * 2 + core
        take(kg_all.at[s], ka_rs.at[s])
        pass_on(s, partner, 11 + off)

    z_take(7, whole, 2)
    z_take(1, whole, 3)
    z_take(4, front, 4)
    z_take(5, whole, 5)
    z_take(4, rear, 6)
    z_take(3, whole, 7)
    for c in range(8):
        s = c * 2 + (1 - core)
        take(kg_all.at[s], ka_rs.at[s])

    for b in range(8):
        take(stat_all.at[b], stat_ss.at[b])
        take(tc_ref.at[b], tc_ss.at[b])
        take(kc_ref.at[b], kc_ss.at[b])
    take(ist_all, ist_ss)
    for b in range(4):
        take(tx_ref.at[b], tx_ss.at[b])
        take(kx_ref.at[b], kx_ss.at[b])
    for j in range(3):
        take(ty_ref.at[j], ty_ss.at[j])
        take(ky_ref.at[j], ky_ss.at[j])
    take(qg_four.at[0:72], qg_ss.at[0])
    take(qg_four.at[72:136], qg_ss.at[1])
    for j in range(6):
        take(qg_recv.at[j], qg_ss.at[2 + j])
    for n, part in enumerate((whole, whole, whole, whole, front, whole, rear, whole)):
        take(qg_all.at[0, part], qa_ss.at[n])
    take(qg_xh, xh_ss)
    for n in range(15):
        take(kg_all.at[n], ka_ss.at[n])


def scoped(*refs):
    pl.run_scoped(
        functools.partial(fused, *refs),
        pltpu.VMEM((576, 2048), BF16),
        pltpu.VMEM((8, 8, 32, 576), BF16),
        pltpu.VMEM((2048, 2048), BF16),
        pltpu.VMEM((1024, 2048), BF16),
        pltpu.VMEM((128, 1024), BF16),
        pltpu.VMEM((2048, 128), BF16),
        pltpu.VMEM((16, 16, 2048), BF16),
        pltpu.VMEM((1024, 2048), BF16),
        pltpu.VMEM((128, 2048), BF16),
    )


def finish(qg_all, kg_all, qg_out, kg_out, wg_out):
    for i in range(8):
        qg_out[i * 128:(i + 1) * 128, :] = qg_all[i, 0:128, :]
        wg_out[i * 2:(i + 1) * 2, :] = qg_all[i, 128:130, 0:64]
    for i in range(16):
        kg_out[i * 128:(i + 1) * 128, :] = kg_all[i]


def shards(main_query, latent_keys, index_query, index_keys, index_weight, query_pos, kl_weight):
    vmem = pl.BlockSpec(memory_space=pltpu.VMEM)
    smem = pl.BlockSpec(memory_space=pltpu.SMEM)
    hbm = pl.BlockSpec(memory_space=pl.ANY)
    dma = pltpu.SemaphoreType.DMA
    query_blocks, key_blocks = pl.pallas_call(
        scoped,
        out_shape=(
            jax.ShapeDtypeStruct((8, 136, 128), F32),
            jax.ShapeDtypeStruct((16, 128, 128), F32),
        ),
        in_specs=[smem, smem, hbm, hbm, vmem, vmem, vmem],
        out_specs=(vmem, vmem),
        scratch_shapes=[
            pltpu.VMEM((8, 576, 256), BF16),
            pltpu.VMEM((576, 2048), BF16),
            pltpu.VMEM((32, 128), F32),
            pltpu.VMEM((256, 2048), F32),
            pltpu.VMEM((256, 2048), F32),
            pltpu.VMEM((256, 128), F32),
            pltpu.VMEM((8, 2, 256), F32),
            pltpu.VMEM((8, 15, 2, 256), F32),
            pltpu.VMEM((8, 2, 16, 2048), F32),
            pltpu.VMEM((8, 16, 2048), F32),
            pltpu.VMEM((4, 16, 2048), F32),
            pltpu.VMEM((3, 16, 2048), F32),
            pltpu.VMEM((128, 128), F32),
            pltpu.VMEM((1024, 128), F32),
            pltpu.VMEM((4, 8, 2048), F32),
            pltpu.VMEM((16, 2048), F32),
            pltpu.VMEM((16, 128), F32),
            pltpu.VMEM((15, 16, 128), F32),
            pltpu.VMEM((128, 128), F32),
            pltpu.VMEM((8, 136, 128), F32),
            pltpu.VMEM((6, 136, 128), F32),
            pltpu.VMEM((136, 128), F32),
            pltpu.VMEM((136, 128), F32),
            pltpu.VMEM((8, 2, 128, 128), F32),
            pltpu.VMEM((8, 128, 128), F32),
            pltpu.VMEM((4, 128, 128), F32),
            pltpu.VMEM((3, 128, 128), F32),
            dma((8,)), dma,
            dma((8,)), dma((8,)), dma, dma,
            dma((8,)), dma((8,)), dma((4,)), dma((4,)), dma((3,)), dma((3,)),
            dma((8,)), dma((8,)), dma, dma, dma((8,)), dma((8,)),
            dma((8,)), dma((8,)), dma((4,)), dma((4,)), dma((3,)), dma((3,)),
            dma((15,)), dma((16,)),
        ],
        compiler_params=pltpu.CompilerParams(
            collective_id=0, has_side_effects=True, vmem_limit_bytes=50 * 1024 * 1024
        ),
        name="fused_indexer_step",
    )(
        query_pos,
        kl_weight,
        jnp.transpose(main_query, (1, 2, 0)),
        jnp.transpose(latent_keys, (1, 0)),
        index_query.reshape(1024, 128),
        index_keys,
        index_weight,
    )
    query_grad, key_grad, weight_grad = pl.pallas_call(
        finish,
        out_shape=(
            jax.ShapeDtypeStruct((1024, 128), F32),
            jax.ShapeDtypeStruct((2048, 128), F32),
            jax.ShapeDtypeStruct((16, 64), F32),
        ),
        in_specs=[vmem, vmem],
        out_specs=(vmem, vmem, vmem),
        compiler_params=pltpu.CompilerParams(vmem_limit_bytes=8 * 1024 * 1024),
        name="finish",
    )(query_blocks, key_blocks)
    return query_grad.reshape(16, 64, 128), key_grad, weight_grad


def solution(mesh):
    placed = (
        P(None, "heads", None),
        P("keys", None),
        P("heads", None, None),
        P("keys", None),
        P("heads", None),
        P(),
        P("heads"),
    )
    return jax.shard_map(
        shards,
        mesh=mesh,
        in_specs=placed,
        out_specs=(P("heads", None, None), P("keys", None), P("heads", None)),
        check_vma=False,
    )
```
